512 devices in a mesh: frame: 32 (over z_lo, x), freq: 16 (over z_hi, y, core).
Axes of the slice: x: 4, y: 4, z: 16 (z_hi: 2, z_lo: 8; z = z_hi * 8 + z_lo), core: 2. Of those that a mesh axis runs over, the one named last changes fastest.
Arguments:
- spectrum: float32 [8192, 16384], P('freq', 'frame'), may hold values from 0.1 to 10
- basis: float32 [8192, 128], P(('freq', 'frame')), may hold values from 0.02 to 0.5
- activations: float32 [16384, 128], P(('frame', 'freq')), may hold values from 0.02 to 0.5
Outputs:
- basis_out: float32 [8192, 128], P(('freq', 'frame'))
- activations_out: float32 [16384, 128], P(('frame', 'freq'))
The draws below stay inside these ranges and needn't reach their ends.
All inputs are finite; a program needn't handle non-finite values.
Results may differ from the reference program's by a relative error of at most 0.0001.
Values sent between devices are 32-bit elements; how exact they have to be, the bound alone decides.
A program may use at most 64 MiB of HBM per device.

```python
import math
import jax
import jax.numpy as jnp
from jax import lax

F = 8192
K = 128
ITERS = 2
FRAMES = 16384


def steps_of(rng, dims, pieces, low, high):
    def one(axis_at, blocks):
        heights = jax.random.uniform(jax.random.fold_in(jax.random.fold_in(rng, 6), axis_at), (blocks,), jnp.float32, low / len(pieces), high / len(pieces))
        return jnp.repeat(jnp.exp(heights), dims[axis_at] // blocks).reshape((-1,) + (1,) * (len(dims) - axis_at - 1))

    factor_of = one(*pieces[0])
    for cut in pieces[1:]:
        factor_of = factor_of * one(*cut)
    return factor_of


def setup_inputs(seed: int = 0) -> dict:
    streams_of = jax.random.split(jax.random.key(seed), 4)
    spectrum = jnp.clip(jnp.exp(math.log(10.0) - 4.6051702 * jax.random.uniform(streams_of[0], (F, FRAMES), jnp.float32) ** steps_of(streams_of[0], (F, FRAMES), ((0, 16), (1, 32)), -0.2, 0.2)), 0.1, 10.0)
    basis = jnp.clip(jnp.exp(math.log(0.5) - 3.218876 * jax.random.uniform(streams_of[1], (F, K), jnp.float32) ** steps_of(streams_of[1], (F, K), ((0, 512),), -0.2, 0.2)), 0.02, 0.5)
    activations = jnp.clip(jnp.exp(math.log(0.5) - 3.218876 * jax.random.uniform(streams_of[2], (FRAMES, K), jnp.float32) ** steps_of(streams_of[2], (FRAMES, K), ((0, 512),), -0.2, 0.2)), 0.02, 0.5)
    return dict(spectrum=spectrum, basis=basis, activations=activations)


def product(left, right, contract_left, contract_right):
    return lax.dot_general(left, right, (((contract_left,), (contract_right,)), ((), ())), precision=lax.Precision.HIGHEST, preferred_element_type=jnp.float32)


def reference(spectrum, basis, activations):
    basis_now = basis
    acts_now = activations
    for sweep in range(ITERS):
        quotient = spectrum / product(basis_now, acts_now, 1, 1)
        basis_total = jnp.sum(basis_now, axis=0)
        acts_now = acts_now * product(quotient, basis_now, 0, 0) / basis_total[None, :]
        quotient = spectrum / product(basis_now, acts_now, 1, 1)
        acts_total = jnp.sum(acts_now, axis=0)
        basis_now = basis_now * product(quotient, acts_now, 1, 0) / acts_total[None, :]
    return basis_now, acts_now
```

```python
import jax
import jax.numpy as jnp
from jax import lax
from jax.experimental import pallas as pl
from jax.experimental.pallas import tpu as pltpu
from jax.sharding import PartitionSpec as P

ITERS = 2
K = 128
X, ZR, ZQ = 4, 4, 2
Y, ZH, C = 4, 2, 2
F32, BF16 = jnp.float32, jnp.bfloat16


def halves(value):
    high = value.astype(BF16)
    return high, (value - high.astype(F32)).astype(BF16)


def dot3(left, right, contract_right):
    dims = (((1,), (contract_right,)), ((), ()))

    def one(a, b):
        return lax.dot_general(a, b, dims, preferred_element_type=F32)

    return one(left[0], right[0]) + (one(left[0], right[1]) + one(left[1], right[0]))


def fold8(value):
    return jnp.sum(value.reshape(value.shape[0] // 8, 8, K), axis=0)


def kernel(
    spec_hbm, basis_ref, acts_ref, basis_out, acts_out,
    spec, spec_t, wp, gp,
    fcore, fcore_in, fy, fy_in, fz, fz_in,
    rx, rx_in, rr, rr_in, rq, rq_in,
    spec_sem, send_sem, recv_sem,
):
    fr = lax.axis_index("frame")
    fq = lax.axis_index("freq")
    x, zl = lax.rem(fr, X), lax.div(fr, X)
    zr, zq = lax.rem(zl, ZR), lax.div(zl, ZR)
    c, yz = lax.rem(fq, C), lax.div(fq, C)
    y, zh = lax.rem(yz, Y), lax.div(yz, Y)
    bins, frames = spec.shape
    wrows, grows = basis_ref.shape[0], acts_ref.shape[0]

    def frame_at(zq_, zr_, x_):
        return ((zq_ * ZR + zr_) * X + x_, fq)

    def freq_at(zh_, y_, c_):
        return (fr, (zh_ * Y + y_) * C + c_)

    def step(value, by, size):
        return lax.rem(value + by, size)

    core_peer = freq_at(zh, y, 1 - c)
    y_peer = {d: freq_at(zh, step(y, d, Y), c) for d in range(1, Y)}
    zh_peer = freq_at(1 - zh, y, c)
    x_peer = {d: frame_at(zq, zr, step(x, d, X)) for d in range(1, X)}
    zr_peer = {d: frame_at(zq, step(zr, d, ZR), x) for d in range(1, ZR)}
    zq_peer = frame_at(1 - zq, zr, x)
    peers = [core_peer, zh_peer, zq_peer, *y_peer.values(), *x_peer.values(), *zr_peer.values()]

    spec_copy = pltpu.make_async_copy(spec_hbm, spec, spec_sem)
    spec_copy.start()

    barrier = pltpu.get_barrier_semaphore()
    for peer in peers:
        pl.semaphore_signal(barrier, inc=1, device_id=peer, device_id_type=pl.DeviceIdType.MESH)

    spec_copy.wait()
    for i in range(frames // 128):
        spec_t[pl.ds(128 * i, 128), :] = spec[:, pl.ds(128 * i, 128)].T

    pl.semaphore_wait(barrier, len(peers))

    copies = []

    def send(src, dst, peer):
        slot = len(copies)
        copy = pltpu.make_async_remote_copy(
            src_ref=src, dst_ref=dst, send_sem=send_sem.at[slot], recv_sem=recv_sem.at[slot],
            device_id=peer, device_id_type=pl.DeviceIdType.MESH,
        )
        copy.start()
        copies.append(copy)
        return copy

    def gather_acts(g):
        mine = g.at[:, y, c]
        near = {d: send(mine, mine, y_peer[d]) for d in (2, 1, 3)}
        waits = [send(mine, mine, core_peer)]
        for d in (1, 3, 2):
            near[d].wait_recv()
            there = g.at[:, step(y, Y - d, Y), c]
            waits.append(send(there, there, core_peer))
        for w in waits:
            w.wait_recv()

    def gather_basis(w):
        mine = w.at[:, zr, x]
        near = {d: send(mine, mine, zr_peer[d]) for d in range(1, ZR)}
        waits = [send(mine, mine, x_peer[d]) for d in (2, 1, 3)]
        for d in range(1, ZR):
            near[d].wait_recv()
            there = w.at[:, step(zr, ZR - d, ZR), x]
            for e in (2, 1, 3):
                waits.append(send(there, there, x_peer[e]))
        for wait in waits:
            wait.wait_recv()

    def reduce_freq(it):
        width = ZH * grows
        first = send(fcore.at[it, 1 - c], fcore_in.at[it], core_peer)
        first.wait_recv()
        total = fcore[it, c] + fcore_in[it]
        for i in range(Y):
            fy[it, i, pl.ds(0, width)] = total[i * width:(i + 1) * width]
            fy[it, i, pl.ds(width, 8)] = total[Y * width:]
        near = {d: send(fy.at[it, step(y, d, Y)], fy_in.at[it, d - 1], y_peer[d]) for d in (2, 1, 3)}
        total = fy[it, y]
        for d in (1, 3, 2):
            near[d].wait_recv()
            total = total + fy_in[it, d - 1]
        fz[it] = total
        far = send(fz.at[it], fz_in.at[it], zh_peer)
        far.wait_recv()
        total = total + fz_in[it]
        return total[:width].reshape(ZH, grows, K), jnp.sum(total[width:], axis=0)

    def reduce_frame(it):
        width = ZQ * wrows
        near = {d: send(rx.at[it, step(x, d, X)], rx_in.at[it, d - 1], x_peer[d]) for d in (2, 1, 3)}
        total = rx[it, x]
        for d in (1, 3, 2):
            near[d].wait_recv()
            total = total + rx_in[it, d - 1]
        for i in range(ZR):
            rr[it, i, pl.ds(0, width)] = total[i * width:(i + 1) * width]
            rr[it, i, pl.ds(width, 8)] = total[ZR * width:]
        near = {d: send(rr.at[it, step(zr, d, ZR)], rr_in.at[it, d - 1], zr_peer[d]) for d in (2, 1, 3)}
        total = rr[it, zr]
        for d in (1, 3, 2):
            near[d].wait_recv()
            total = total + rr_in[it, d - 1]
        rq[it] = total
        far = send(rq.at[it], rq_in.at[it], zq_peer)
        far.wait_recv()
        total = total + rq_in[it]
        return total[:width].reshape(ZQ, wrows, K), jnp.sum(total[width:], axis=0)

    far_acts = send(acts_ref, gp.at[0, zh, y, c], zh_peer)
    far_basis = send(basis_ref, wp.at[0, zq, zr, x], zq_peer)
    gp[0, zh, y, c] = acts_ref[...]
    wp[0, zq, zr, x] = basis_ref[...]
    far_basis.wait_recv()
    gather_basis(wp.at[0])
    far_acts.wait_recv()
    gather_acts(gp.at[0])

    rows = 128
    for it in range(ITERS):
        w_now = wp[it].reshape(bins, K)
        g_now = gp[it].reshape(frames, K)
        wh = halves(w_now)
        gh = halves(g_now)
        sums = fold8(w_now)
        for j in range(C):
            fcore[it, j, pl.ds(Y * ZH * grows, 8)] = sums
        for i in range(frames // rows):
            at = slice(i * rows, (i + 1) * rows)
            product = dot3((gh[0][at], gh[1][at]), wh, 1)
            quotient = spec_t[pl.ds(i * rows, rows), :] / product
            terms = dot3(halves(quotient), wh, 0)
            for b in range(rows // grows):
                q = i * (rows // grows) + b
                cc, yy, zz = q % C, (q // C) % Y, q // (C * Y)
                fcore[it, cc, pl.ds((yy * ZH + zz) * grows, grows)] = terms[b * grows:(b + 1) * grows]
        numerator, total = reduce_freq(it)
        fresh = gp[it, :, y, c] * numerator / total
        gp[it + 1, :, y, c] = fresh
        gather_acts(gp.at[it + 1])
        if it + 1 == ITERS:
            acts_out[...] = gp[it + 1, zh, y, c]

        g_now = gp[it + 1].reshape(frames, K)
        gh = halves(g_now)
        sums = fold8(g_now)
        for j in range(X):
            rx[it, j, pl.ds(ZR * ZQ * wrows, 8)] = sums
        for i in range(bins // rows):
            at = slice(i * rows, (i + 1) * rows)
            product = dot3((wh[0][at], wh[1][at]), gh, 1)
            quotient = spec[pl.ds(i * rows, rows), :] / product
            terms = dot3(halves(quotient), gh, 0)
            for b in range(rows // wrows):
                q = i * (rows // wrows) + b
                xx, rr_, qq = q % X, (q // X) % ZR, q // (X * ZR)
                rx[it, xx, pl.ds((rr_ * ZQ + qq) * wrows, wrows)] = terms[b * wrows:(b + 1) * wrows]
        numerator, total = reduce_frame(it)
        fresh = wp[it, :, zr, x] * numerator / total
        wp[it + 1, :, zr, x] = fresh
        if it + 1 < ITERS:
            gather_basis(wp.at[it + 1])
        else:
            basis_out[...] = wp[it + 1, zq, zr, x]

    for copy in copies:
        copy.wait_send()


def per_device(spectrum, basis, activations):
    bins, frames = spectrum.shape
    wrows, grows = basis.shape[0], activations.shape[0]
    fwide, rwide = Y * ZH * grows + 8, ZR * ZQ * wrows + 8
    fpart, rpart = ZH * grows + 8, ZQ * wrows + 8
    vmem = pl.BlockSpec(memory_space=pltpu.VMEM)
    return pl.pallas_call(
        kernel,
        out_shape=(
            jax.ShapeDtypeStruct(basis.shape, F32),
            jax.ShapeDtypeStruct(activations.shape, F32),
        ),
        in_specs=[pl.BlockSpec(memory_space=pl.ANY), vmem, vmem],
        out_specs=(vmem, vmem),
        scratch_shapes=[
            pltpu.VMEM((bins, frames), F32),
            pltpu.VMEM((frames, bins), F32),
            pltpu.VMEM((ITERS + 1, ZQ, ZR, X, wrows, K), F32),
            pltpu.VMEM((ITERS + 1, ZH, Y, C, grows, K), F32),
            pltpu.VMEM((ITERS, C, fwide, K), F32),
            pltpu.VMEM((ITERS, fwide, K), F32),
            pltpu.VMEM((ITERS, Y, fpart, K), F32),
            pltpu.VMEM((ITERS, Y - 1, fpart, K), F32),
            pltpu.VMEM((ITERS, fpart, K), F32),
            pltpu.VMEM((ITERS, fpart, K), F32),
            pltpu.VMEM((ITERS, X, rwide, K), F32),
            pltpu.VMEM((ITERS, X - 1, rwide, K), F32),
            pltpu.VMEM((ITERS, ZR, rpart, K), F32),
            pltpu.VMEM((ITERS, ZR - 1, rpart, K), F32),
            pltpu.VMEM((ITERS, rpart, K), F32),
            pltpu.VMEM((ITERS, rpart, K), F32),
            pltpu.SemaphoreType.DMA(()),
            pltpu.SemaphoreType.DMA((96,)),
            pltpu.SemaphoreType.DMA((96,)),
        ],
        compiler_params=pltpu.CompilerParams(
            collective_id=0, has_side_effects=True, vmem_limit_bytes=48 * 1024 * 1024
        ),
    )(spectrum, basis, activations)


def solution(mesh):
    return jax.shard_map(
        per_device,
        mesh=mesh,
        in_specs=(P("freq", "frame"), P(("freq", "frame"), None), P(("frame", "freq"), None)),
        out_specs=(P(("freq", "frame"), None), P(("frame", "freq"), None)),
        check_vma=False,
    )
```

```python
import jax
import jax.numpy as jnp
from jax import lax
from jax.experimental import pallas as pl
from jax.experimental.pallas import tpu as pltpu
from jax.sharding import PartitionSpec as P

ITERS = 2
K = 128
X, ZR, ZQ = 4, 4, 2
Y, ZH, C = 4, 2, 2
SEMS = 160
F32, BF16 = jnp.float32, jnp.bfloat16


def halves(value):
    high = value.astype(BF16)
    return high, (value - high.astype(F32)).astype(BF16)


def dot(left, right, contract_right):
    return lax.dot_general(
        left, right, (((1,), (contract_right,)), ((), ())), preferred_element_type=F32
    )


def outer(left, right):
    wide = dot(jnp.concatenate(left, axis=1), jnp.concatenate([right[0], right[0]], axis=1), 1)
    return wide + dot(left[0], right[1], 1)


def inner(left, right):
    wide = dot(left[0], jnp.concatenate(right, axis=1), 0)
    return wide[:, :K] + wide[:, K:] + dot(left[1], right[0], 0)


def fold8(value):
    return jnp.sum(value.reshape(-1, 8, K), axis=0)


def kernel(
    spec_hbm, basis_hbm, acts_hbm, basis_out, acts_out,
    raw, spec, spec_t, wp, gp,
    fcore, fcore_in, fy, fy_in, fz, fz_in,
    wacc, rx, rx_in, rs, rs_in, rq, rq_in,
    load_sem, send_sem, recv_sem,
):
    fr = lax.axis_index("frame")
    fq = lax.axis_index("freq")
    x, zl = lax.rem(fr, X), lax.div(fr, X)
    zr, zq = lax.rem(zl, ZR), lax.div(zl, ZR)
    c, yz = lax.rem(fq, C), lax.div(fq, C)
    y, zh = lax.rem(yz, Y), lax.div(yz, Y)
    wrows, grows = basis_hbm.shape[0], acts_hbm.shape[0]
    xbins, cframes = ZQ * ZR * wrows, ZH * Y * grows
    gpart, wpart = ZH * grows, ZQ * wrows

    def frame_at(zq_, zr_, x_):
        return ((zq_ * ZR + zr_) * X + x_, fq)

    def freq_at(zh_, y_, c_):
        return (fr, (zh_ * Y + y_) * C + c_)

    def step(value, by, size):
        return lax.rem(value + by, size)

    core_peer = freq_at(zh, y, 1 - c)
    zh_peer = freq_at(1 - zh, y, c)
    zq_peer = frame_at(1 - zq, zr, x)
    y_peer = {d: freq_at(zh, step(y, d, Y), c) for d in (2, 1, 3)}
    steps = [(d, e) for d in (2, 1, 3, 0) for e in (2, 1, 3, 0) if d or e]
    xz_peer = {(d, e): frame_at(zq, step(zr, e, ZR), step(x, d, X)) for d, e in steps}
    peers = [core_peer, zh_peer, zq_peer, *y_peer.values(), *xz_peer.values()]

    loads = [
        pltpu.make_async_copy(basis_hbm, wp.at[0, x, zq, zr], load_sem.at[0]),
        pltpu.make_async_copy(acts_hbm, gp.at[0, c, zh, y], load_sem.at[1]),
    ]
    for i in range(X):
        loads.append(pltpu.make_async_copy(spec_hbm.at[:, i], raw.at[i], load_sem.at[2 + i]))
    for load in loads:
        load.start()

    barrier = pltpu.get_barrier_semaphore()
    for peer in peers:
        pl.semaphore_signal(barrier, inc=1, device_id=peer, device_id_type=pl.DeviceIdType.MESH)

    for load in loads:
        load.wait()
    for i in range(X):
        turned = raw[i].reshape(xbins, C * cframes).T
        for j in range(C * ZH * Y):
            spec_t[i, j % C, pl.ds(j // C * grows, grows)] = turned[j * grows:(j + 1) * grows]
    for i in range(X):
        for j in range(C):
            spec[j, i] = spec_t[i, j].T

    pl.semaphore_wait(barrier, len(peers))

    copies = []

    def send(src, dst, peer):
        slot = len(copies)
        copy = pltpu.make_async_remote_copy(
            src_ref=src, dst_ref=dst, send_sem=send_sem.at[slot], recv_sem=recv_sem.at[slot],
            device_id=peer, device_id_type=pl.DeviceIdType.MESH,
        )
        copy.start()
        copies.append(copy)
        return copy

    def send_near(ref):
        return {d: send(ref, ref, y_peer[d]) for d in (2, 1, 3)}

    def send_plane(ref):
        return {at: send(ref, ref, xz_peer[at]) for at in steps}

    def wait_all(waits):
        for wait in waits:
            wait.wait_recv()

    def wait_near(near, part):
        passed = []
        for d in (1, 3, 2):
            near[d].wait_recv()
            there = part(step(y, Y - d, Y))
            passed.append(send(there, there, core_peer))
        return passed

    mine_w, mine_g = wp.at[0, x, zq, zr], gp.at[0, c, zh, y]
    far_g = send(mine_g, mine_g, zh_peer)
    far_w = send(mine_w, mine_w, zq_peer)
    near = send_near(mine_g)
    cross = [send(mine_g, mine_g, core_peer)]
    plane = send_plane(mine_w)
    cross += wait_near(near, lambda y_: gp.at[0, c, zh, y_])
    far_w.wait_recv()
    there = wp.at[0, x, 1 - zq, zr]
    plane_far = send_plane(there)
    far_g.wait_recv()
    there = gp.at[0, c, 1 - zh, y]
    near = send_near(there)
    cross.append(send(there, there, core_peer))
    wait_all(plane.values())
    wait_all(plane_far.values())
    cross += wait_near(near, lambda y_: gp.at[0, c, 1 - zh, y_])
    wait_all(cross)
    plane = None

    def acts_terms(it, c_, zh_, xs):
        w = halves(jnp.concatenate([wp[it, i].reshape(xbins, K) for i in xs], axis=0))
        g = halves(gp[it, c_, zh_].reshape(Y * grows, K))
        rows = pl.ds(zh_ * Y * grows, Y * grows)
        s = jnp.concatenate([spec_t[i, c_, rows] for i in xs], axis=1)
        return inner(halves(s / outer(g, w)), w)

    def basis_terms(it, x_, c_):
        w = halves(wp[it, x_].reshape(xbins, K))
        g = halves(gp[it + 1, c_].reshape(cframes, K))
        return inner(halves(spec[c_, x_] / outer(w, g)), g)

    for it in range(ITERS):
        if plane is not None:
            wait_all(plane[0, e] for e in range(1, ZR))
        for c_ in range(C):
            for zh_ in range(ZH):
                rows = pl.ds(zh_ * Y * grows, Y * grows)
                fcore[it, c_, rows] = acts_terms(it, c_, zh_, [x])
        if plane is not None:
            wait_all(plane[at] for at in steps if at[0])
        sums = fold8(wp[it])
        for c_ in range(C):
            fcore[it, c_, pl.ds(cframes, 8)] = sums
        others = [step(x, d, X) for d in (1, 3, 2)]
        for c_ in (1 - c, c):
            for zh_ in range(ZH):
                rows = pl.ds(zh_ * Y * grows, Y * grows)
                fcore[it, c_, rows] += acts_terms(it, c_, zh_, others)
            if c_ is not c:
                first = send(fcore.at[it, c_], fcore_in.at[it], core_peer)
        first.wait_recv()
        total = fcore[it, c] + fcore_in[it]
        for i in range(Y):
            for j in range(ZH):
                at = (j * Y + i) * grows
                fy[it, i, pl.ds(j * grows, grows)] = total[at:at + grows]
            fy[it, i, pl.ds(gpart, 8)] = total[cframes:]
        near = {d: send(fy.at[it, step(y, d, Y)], fy_in.at[it, d - 1], y_peer[d]) for d in (2, 1, 3)}
        total = fy[it, y]
        for d in (1, 3, 2):
            near[d].wait_recv()
            total = total + fy_in[it, d - 1]
        fz[it] = total
        far = send(fz.at[it], fz_in.at[it], zh_peer)
        far.wait_recv()
        total = total + fz_in[it]
        scale = jnp.sum(total[gpart:], axis=0)
        gp[it + 1, c, :, y] = gp[it, c, :, y] * total[:gpart].reshape(ZH, grows, K) / scale
        mine = gp.at[it + 1, c, :, y]
        near = send_near(mine)
        cross = [send(mine, mine, core_peer)]
        if it + 1 == ITERS:
            acts_out[...] = gp[it + 1, c, zh, y]
        cross += wait_near(near, lambda y_: gp.at[it + 1, c, :, y_])

        for i in range(X):
            wacc[i] = basis_terms(it, i, c)
        sums = fold8(gp[it + 1, c])
        wait_all(cross)
        sums = sums + fold8(gp[it + 1, 1 - c])
        rs[it] = sums
        totals = {at: send(rs.at[it], rs_in.at[it, at[0], at[1]], xz_peer[at]) for at in steps}
        plane = {}
        for d in (2, 1, 3, 0):
            x_ = step(x, d, X)
            terms = wacc[x_] + basis_terms(it, x_, 1 - c)
            for i in range(ZR):
                for j in range(ZQ):
                    at = (j * ZR + i) * wrows
                    rx[it, x_, i, pl.ds(j * wrows, wrows)] = terms[at:at + wrows]
            for at in steps:
                if at[0] == d:
                    src = rx.at[it, x_, step(zr, at[1], ZR)]
                    plane[at] = send(src, rx_in.at[it, at[0], at[1]], xz_peer[at])
        for at in steps:
            totals[at].wait_recv()
            sums = sums + rs_in[it, at[0], at[1]]
        total = rx[it, x, zr]
        for at in sorted(steps):
            plane[at].wait_recv()
            total = total + rx_in[it, at[0], at[1]]
        rq[it, pl.ds(0, wpart)] = total
        rq[it, pl.ds(wpart, 8)] = sums
        far = send(rq.at[it], rq_in.at[it], zq_peer)
        far.wait_recv()
        total = (total + rq_in[it, pl.ds(0, wpart)]).reshape(ZQ, wrows, K)
        scale = jnp.sum(sums + rq_in[it, pl.ds(wpart, 8)], axis=0)
        wp[it + 1, x, :, zr] = wp[it, x, :, zr] * total / scale
        if it + 1 < ITERS:
            plane = send_plane(wp.at[it + 1, x, :, zr])
        else:
            basis_out[...] = wp[it + 1, x, zq, zr]

    for copy in copies:
        copy.wait_send()


def per_device(spectrum, basis, activations):
    bins, frames = spectrum.shape
    wrows, grows = basis.shape[0], activations.shape[0]
    gpart, wpart = ZH * grows, ZQ * wrows
    fwide = Y * gpart + 8
    anywhere = pl.BlockSpec(memory_space=pl.ANY)
    vmem = pl.BlockSpec(memory_space=pltpu.VMEM)
    return pl.pallas_call(
        kernel,
        out_shape=(
            jax.ShapeDtypeStruct(basis.shape, F32),
            jax.ShapeDtypeStruct(activations.shape, F32),
        ),
        in_specs=[anywhere] * 3,
        out_specs=(vmem, vmem),
        scratch_shapes=[
            pltpu.VMEM((X, ZQ * ZR, wrows, frames), F32),
            pltpu.VMEM((C, X, bins // X, frames // C), F32),
            pltpu.VMEM((X, C, frames // C, bins // X), F32),
            pltpu.VMEM((ITERS + 1, X, ZQ, ZR, wrows, K), F32),
            pltpu.VMEM((ITERS + 1, C, ZH, Y, grows, K), F32),
            pltpu.VMEM((ITERS, C, fwide, K), F32),
            pltpu.VMEM((ITERS, fwide, K), F32),
            pltpu.VMEM((ITERS, Y, gpart + 8, K), F32),
            pltpu.VMEM((ITERS, Y - 1, gpart + 8, K), F32),
            pltpu.VMEM((ITERS, gpart + 8, K), F32),
            pltpu.VMEM((ITERS, gpart + 8, K), F32),
            pltpu.VMEM((X, bins // X, K), F32),
            pltpu.VMEM((ITERS, X, ZR, wpart, K), F32),
            pltpu.VMEM((ITERS, X, ZR, wpart, K), F32),
            pltpu.VMEM((ITERS, 8, K), F32),
            pltpu.VMEM((ITERS, X, ZR, 8, K), F32),
            pltpu.VMEM((ITERS, wpart + 8, K), F32),
            pltpu.VMEM((ITERS, wpart + 8, K), F32),
            pltpu.SemaphoreType.DMA((2 + X,)),
            pltpu.SemaphoreType.DMA((SEMS,)),
            pltpu.SemaphoreType.DMA((SEMS,)),
        ],
        compiler_params=pltpu.CompilerParams(
            collective_id=0, has_side_effects=True, vmem_limit_bytes=67_043_328
        ),
    )(spectrum.reshape(ZQ * ZR, X, wrows, frames), basis, activations)


def solution(mesh):
    return jax.shard_map(
        per_device,
        mesh=mesh,
        in_specs=(P("freq", "frame"), P(("freq", "frame"), None), P(("frame", "freq"), None)),
        out_specs=(P(("freq", "frame"), None), P(("frame", "freq"), None)),
        check_vma=False,
    )
```

```python
import jax
import jax.numpy as jnp
from jax import lax
from jax.experimental import pallas as pl
from jax.experimental.pallas import tpu as pltpu
from jax.sharding import PartitionSpec as P

ITERS = 2
K = 128
X, ZR, ZQ = 4, 4, 2
Y, ZH, C = 4, 2, 2
SEMS = 160
F32, BF16 = jnp.float32, jnp.bfloat16


def halves(value):
    high = value.astype(BF16)
    return high, (value - high.astype(F32)).astype(BF16)


def dot(left, right, contract_right):
    return lax.dot_general(
        left, right, (((1,), (contract_right,)), ((), ())), preferred_element_type=F32
    )


def outer(left, right):
    wide = dot(jnp.concatenate(left, axis=1), jnp.concatenate([right[0], right[0]], axis=1), 1)
    return wide + dot(left[0], right[1], 1)


def inner(left, right):
    wide = dot(left[0], jnp.concatenate(right, axis=1), 0)
    return wide[:, :K] + wide[:, K:] + dot(left[1], right[0], 0)


def fold8(value):
    return jnp.sum(value.reshape(-1, 8, K), axis=0)


def kernel(
    spec_hbm, basis_hbm, acts_hbm, basis_out, acts_out,
    raw, spec, spec_t, wp, gp,
    fcore, fcore_in, fy, fy_in, fz, fz_in,
    wacc, rx, rx_in, rs, rs_in, rq, rq_in,
    load_sem, send_sem, recv_sem,
):
    fr = lax.axis_index("frame")
    fq = lax.axis_index("freq")
    x, zl = lax.rem(fr, X), lax.div(fr, X)
    zr, zq = lax.rem(zl, ZR), lax.div(zl, ZR)
    c, yz = lax.rem(fq, C), lax.div(fq, C)
    y, zh = lax.rem(yz, Y), lax.div(yz, Y)
    wrows, grows = basis_hbm.shape[0], acts_hbm.shape[0]
    xbins, cframes = ZQ * ZR * wrows, ZH * Y * grows
    gpart, wpart = ZH * grows, ZQ * wrows

    def frame_at(zq_, zr_, x_):
        return ((zq_ * ZR + zr_) * X + x_, fq)

    def freq_at(zh_, y_, c_):
        return (fr, (zh_ * Y + y_) * C + c_)

    def step(value, by, size):
        return lax.rem(value + by, size)

    core_peer = freq_at(zh, y, 1 - c)
    zh_peer = freq_at(1 - zh, y, c)
    zq_peer = frame_at(1 - zq, zr, x)
    y_peer = {d: freq_at(zh, step(y, d, Y), c) for d in (2, 1, 3)}
    steps = [(d, e) for d in (2, 1, 3, 0) for e in (2, 1, 3, 0) if d or e]
    xz_peer = {(d, e): frame_at(zq, step(zr, e, ZR), step(x, d, X)) for d, e in steps}
    peers = [zh_peer, zq_peer, *xz_peer.values(), *y_peer.values(), core_peer]

    barrier = pltpu.get_barrier_semaphore()
    for peer in peers:
        pl.semaphore_signal(barrier, inc=1, device_id=peer, device_id_type=pl.DeviceIdType.MESH)

    loads = [
        pltpu.make_async_copy(acts_hbm, gp.at[0, c, zh, y], load_sem.at[0]),
        pltpu.make_async_copy(basis_hbm, wp.at[0, x, zq, zr], load_sem.at[1]),
    ]
    for i in range(X):
        loads.append(pltpu.make_async_copy(spec_hbm.at[:, i], raw.at[i], load_sem.at[2 + i]))
    for load in loads:
        load.start()
    loads[0].wait()
    loads[1].wait()
    pl.semaphore_wait(barrier, len(peers))

    copies = []

    def send(src, dst, peer):
        slot = len(copies)
        copy = pltpu.make_async_remote_copy(
            src_ref=src, dst_ref=dst, send_sem=send_sem.at[slot], recv_sem=recv_sem.at[slot],
            device_id=peer, device_id_type=pl.DeviceIdType.MESH,
        )
        copy.start()
        copies.append(copy)
        return copy

    def send_near(ref):
        return {d: send(ref, ref, y_peer[d]) for d in (2, 1, 3)}

    def send_plane(ref):
        return {at: send(ref, ref, xz_peer[at]) for at in steps}

    def wait_all(waits):
        for wait in waits:
            wait.wait_recv()

    def wait_near(near, part):
        passed = []
        for d in (1, 3, 2):
            near[d].wait_recv()
            there = part(step(y, Y - d, Y))
            passed.append(send(there, there, core_peer))
        return passed

    mine_w, mine_g = wp.at[0, x, zq, zr], gp.at[0, c, zh, y]
    far_g = send(mine_g, mine_g, zh_peer)
    far_w = send(mine_w, mine_w, zq_peer)
    near = send_near(mine_g)
    cross = [send(mine_g, mine_g, core_peer)]
    plane = send_plane(mine_w)
    for load in loads[2:]:
        load.wait()
    for i in range(X):
        turned = raw[i].reshape(xbins, C * cframes).T
        for j in range(C * ZH * Y):
            spec_t[i, j % C, pl.ds(j // C * grows, grows)] = turned[j * grows:(j + 1) * grows]
    cross += wait_near(near, lambda y_: gp.at[0, c, zh, y_])
    far_w.wait_recv()
    there = wp.at[0, x, 1 - zq, zr]
    plane_far = send_plane(there)
    far_g.wait_recv()
    wait_all(cross)
    there = gp.at[0, c, 1 - zh, y]
    near = send_near(there)
    cross = [send(there, there, core_peer)]
    wait_all(plane.values())
    wait_all(plane_far.values())
    plane = None

    def acts_terms(it, c_, zh_, xs):
        w = halves(jnp.concatenate([wp[it, i].reshape(xbins, K) for i in xs], axis=0))
        g = halves(gp[it, c_, zh_].reshape(Y * grows, K))
        rows = pl.ds(zh_ * Y * grows, Y * grows)
        s = jnp.concatenate([spec_t[i, c_, rows] for i in xs], axis=1)
        return inner(halves(s / outer(g, w)), w)

    def basis_terms(it, x_, c_):
        w = halves(wp[it, x_].reshape(xbins, K))
        g = halves(gp[it + 1, c_].reshape(cframes, K))
        return inner(halves(spec[c_, x_] / outer(w, g)), g)

    for it in range(ITERS):
        def add_terms(c_, zh_, xs, fresh):
            rows = pl.ds(zh_ * Y * grows, Y * grows)
            terms = acts_terms(it, c_, zh_, xs)
            fcore[it, c_, rows] = terms if fresh else fcore[it, c_, rows] + terms

        sides = [(1 - c, zh), (c, zh), (1 - c, 1 - zh), (c, 1 - zh)]
        others = [step(x, d, X) for d in (1, 3, 2)]
        if it == 0:
            for side in sides[:2]:
                add_terms(*side, [x, *others], True)
            cross += wait_near(near, lambda y_: gp.at[0, c, 1 - zh, y_])
            wait_all(cross)
        else:
            wait_all(plane[0, e] for e in range(1, ZR))
            for side in sides:
                add_terms(*side, [x], True)
            wait_all(plane[at] for at in steps if at[0])
        sums = fold8(wp[it])
        for c_ in range(C):
            fcore[it, c_, pl.ds(cframes, 8)] = sums
        for i in (2, 0, 3, 1):
            if it:
                add_terms(*sides[i], others, False)
            elif i >= 2:
                add_terms(*sides[i], [x, *others], True)
            if i == (0 if it else 2):
                first = send(fcore.at[it, 1 - c], fcore_in.at[it], core_peer)
        first.wait_recv()
        total = fcore[it, c] + fcore_in[it]
        for i in range(Y):
            for j in range(ZH):
                at = (j * Y + i) * grows
                fy[it, i, pl.ds(j * grows, grows)] = total[at:at + grows]
            fy[it, i, pl.ds(gpart, 8)] = total[cframes:]
        near = {d: send(fy.at[it, step(y, d, Y)], fy_in.at[it, d - 1], y_peer[d]) for d in (2, 1, 3)}
        total = fy[it, y]
        for d in (1, 3, 2):
            near[d].wait_recv()
            total = total + fy_in[it, d - 1]
        fz[it] = total
        far = send(fz.at[it], fz_in.at[it], zh_peer)
        if it == 0:
            for i in range(X):
                for j in range(C):
                    spec[j, i] = spec_t[i, j].T
        far.wait_recv()
        total = total + fz_in[it]
        scale = jnp.sum(total[gpart:], axis=0)
        gp[it + 1, c, :, y] = gp[it, c, :, y] * total[:gpart].reshape(ZH, grows, K) / scale
        mine = gp.at[it + 1, c, :, y]
        near = send_near(mine)
        cross = [send(mine, mine, core_peer)]
        if it + 1 == ITERS:
            acts_out[...] = gp[it + 1, c, zh, y]
        cross += wait_near(near, lambda y_: gp.at[it + 1, c, :, y_])

        for i in range(X):
            wacc[i] = basis_terms(it, i, c)
        sums = fold8(gp[it + 1, c])
        wait_all(cross)
        sums = sums + fold8(gp[it + 1, 1 - c])
        rs[it] = sums
        totals = {at: send(rs.at[it], rs_in.at[it, at[0], at[1]], xz_peer[at]) for at in steps}
        plane = {}
        for d in (2, 1, 3, 0):
            x_ = step(x, d, X)
            terms = wacc[x_] + basis_terms(it, x_, 1 - c)
            for i in range(ZR):
                for j in range(ZQ):
                    at = (j * ZR + i) * wrows
                    rx[it, x_, i, pl.ds(j * wrows, wrows)] = terms[at:at + wrows]
            for at in steps:
                if at[0] == d:
                    src = rx.at[it, x_, step(zr, at[1], ZR)]
                    plane[at] = send(src, rx_in.at[it, at[0], at[1]], xz_peer[at])
        for at in steps:
            totals[at].wait_recv()
            sums = sums + rs_in[it, at[0], at[1]]
        total = rx[it, x, zr]
        for at in sorted(steps):
            plane[at].wait_recv()
            total = total + rx_in[it, at[0], at[1]]
        rq[it, pl.ds(0, wpart)] = total
        rq[it, pl.ds(wpart, 8)] = sums
        far = send(rq.at[it], rq_in.at[it], zq_peer)
        far.wait_recv()
        total = (total + rq_in[it, pl.ds(0, wpart)]).reshape(ZQ, wrows, K)
        scale = jnp.sum(sums + rq_in[it, pl.ds(wpart, 8)], axis=0)
        wp[it + 1, x, :, zr] = wp[it, x, :, zr] * total / scale
        if it + 1 < ITERS:
            plane = send_plane(wp.at[it + 1, x, :, zr])
        else:
            basis_out[...] = wp[it + 1, x, zq, zr]

    for copy in copies:
        copy.wait_send()


def per_device(spectrum, basis, activations):
    bins, frames = spectrum.shape
    wrows, grows = basis.shape[0], activations.shape[0]
    gpart, wpart = ZH * grows, ZQ * wrows
    fwide = Y * gpart + 8
    anywhere = pl.BlockSpec(memory_space=pl.ANY)
    vmem = pl.BlockSpec(memory_space=pltpu.VMEM)
    return pl.pallas_call(
        kernel,
        out_shape=(
            jax.ShapeDtypeStruct(basis.shape, F32),
            jax.ShapeDtypeStruct(activations.shape, F32),
        ),
        in_specs=[anywhere] * 3,
        out_specs=(vmem, vmem),
        scratch_shapes=[
            pltpu.VMEM((X, ZQ * ZR, wrows, frames), F32),
            pltpu.VMEM((C, X, bins // X, frames // C), F32),
            pltpu.VMEM((X, C, frames // C, bins // X), F32),
            pltpu.VMEM((ITERS + 1, X, ZQ, ZR, wrows, K), F32),
            pltpu.VMEM((ITERS + 1, C, ZH, Y, grows, K), F32),
            pltpu.VMEM((ITERS, C, fwide, K), F32),
            pltpu.VMEM((ITERS, fwide, K), F32),
            pltpu.VMEM((ITERS, Y, gpart + 8, K), F32),
            pltpu.VMEM((ITERS, Y - 1, gpart + 8, K), F32),
            pltpu.VMEM((ITERS, gpart + 8, K), F32),
            pltpu.VMEM((ITERS, gpart + 8, K), F32),
            pltpu.VMEM((X, bins // X, K), F32),
            pltpu.VMEM((ITERS, X, ZR, wpart, K), F32),
            pltpu.VMEM((ITERS, X, ZR, wpart, K), F32),
            pltpu.VMEM((ITERS, 8, K), F32),
            pltpu.VMEM((ITERS, X, ZR, 8, K), F32),
            pltpu.VMEM((ITERS, wpart + 8, K), F32),
            pltpu.VMEM((ITERS, wpart + 8, K), F32),
            pltpu.SemaphoreType.DMA((2 + X,)),
            pltpu.SemaphoreType.DMA((SEMS,)),
            pltpu.SemaphoreType.DMA((SEMS,)),
        ],
        compiler_params=pltpu.CompilerParams(
            collective_id=0, has_side_effects=True, vmem_limit_bytes=67_043_328
        ),
    )(spectrum.reshape(ZQ * ZR, X, wrows, frames), basis, activations)


def solution(mesh):
    return jax.shard_map(
        per_device,
        mesh=mesh,
        in_specs=(P("freq", "frame"), P(("freq", "frame"), None), P(("frame", "freq"), None)),
        out_specs=(P(("freq", "frame"), None), P(("frame", "freq"), None)),
        check_vma=False,
    )
```

```python
import jax
import jax.numpy as jnp
from jax import lax
from jax.experimental import pallas as pl
from jax.experimental.pallas import tpu as pltpu
from jax.sharding import PartitionSpec as P

ITERS = 2
K = 128
X, ZR, ZQ = 4, 4, 2
Y, ZH, C = 4, 2, 2
SEMS = 160
GROUP = 2
PAIRS = ((2, 1), (3, 0))
F32, BF16 = jnp.float32, jnp.bfloat16


def halves(value):
    high = value.astype(BF16)
    return high, (value - high.astype(F32)).astype(BF16)


def dot(left, right, contract_right):
    return lax.dot_general(
        left, right, (((1,), (contract_right,)), ((), ())), preferred_element_type=F32
    )


def outer(left, right):
    wide = dot(jnp.concatenate(left, axis=1), jnp.concatenate([right[0], right[0]], axis=1), 1)
    return wide + dot(left[0], right[1], 1)


def inner(left, right):
    wide = dot(left[0], jnp.concatenate(right, axis=1), 0)
    return wide[:, :K] + wide[:, K:] + dot(left[1], right[0], 0)


def fold8(value):
    return jnp.sum(value.reshape(-1, 8, K), axis=0)


def kernel(
    spec_hbm, basis_hbm, acts_hbm, basis_out, acts_out,
    raw, spec, spec_t, wp, gp,
    fcore, fcore_in, fy, fy_in, fz, fz_in,
    wacc, rx, rx_in, rs, rs_in, rq, rq_in,
    load_sem, send_sem, recv_sem,
):
    fr = lax.axis_index("frame")
    fq = lax.axis_index("freq")
    x, zl = lax.rem(fr, X), lax.div(fr, X)
    zr, zq = lax.rem(zl, ZR), lax.div(zl, ZR)
    c, yz = lax.rem(fq, C), lax.div(fq, C)
    y, zh = lax.rem(yz, Y), lax.div(yz, Y)
    wrows, grows = basis_hbm.shape[0], acts_hbm.shape[0]
    xbins, cframes = ZQ * ZR * wrows, ZH * Y * grows
    gpart, wpart = ZH * grows, ZQ * wrows

    def frame_at(zq_, zr_, x_):
        return ((zq_ * ZR + zr_) * X + x_, fq)

    def freq_at(zh_, y_, c_):
        return (fr, (zh_ * Y + y_) * C + c_)

    def step(value, by, size):
        return lax.rem(value + by, size)

    core_peer = freq_at(zh, y, 1 - c)
    zh_peer = freq_at(1 - zh, y, c)
    zq_peer = frame_at(1 - zq, zr, x)
    y_peer = {d: freq_at(zh, step(y, d, Y), c) for d in (2, 1, 3)}
    steps = [(d, e) for d in (2, 1, 3, 0) for e in (2, 1, 3, 0) if d or e]
    xz_peer = {(d, e): frame_at(zq, step(zr, e, ZR), step(x, d, X)) for d, e in steps}
    peers = [zh_peer, zq_peer, *xz_peer.values(), *y_peer.values(), core_peer]

    barrier = pltpu.get_barrier_semaphore()
    for peer in peers:
        pl.semaphore_signal(barrier, inc=1, device_id=peer, device_id_type=pl.DeviceIdType.MESH)

    loads = [
        pltpu.make_async_copy(acts_hbm, gp.at[0, c, zh, y], load_sem.at[0]),
        pltpu.make_async_copy(basis_hbm, wp.at[0, x, zq, zr], load_sem.at[1]),
    ]
    for i in range(X):
        loads.append(pltpu.make_async_copy(spec_hbm.at[:, i], raw.at[i], load_sem.at[2 + i]))
    for load in loads:
        load.start()
    loads[0].wait()
    loads[1].wait()
    pl.semaphore_wait(barrier, len(peers))

    copies, drained = [], []

    def drain():
        for copy in copies[len(drained):-1]:
            copy.wait_send()
            drained.append(copy)

    def send(src, dst, peer):
        slot = len(copies)
        copy = pltpu.make_async_remote_copy(
            src_ref=src, dst_ref=dst, send_sem=send_sem.at[slot], recv_sem=recv_sem.at[slot],
            device_id=peer, device_id_type=pl.DeviceIdType.MESH,
        )
        copy.start()
        copies.append(copy)
        return copy

    def send_near(ref):
        return {d: send(ref, ref, y_peer[d]) for d in (2, 1, 3)}

    def send_plane(ref):
        return {at: send(ref, ref, xz_peer[at]) for at in steps}

    def wait_all(waits):
        for wait in waits:
            wait.wait_recv()

    def wait_near(near, part):
        passed = []
        for d in (1, 3, 2):
            near[d].wait_recv()
            there = part(step(y, Y - d, Y))
            passed.append(send(there, there, core_peer))
        return passed

    mine_w, mine_g = wp.at[0, x, zq, zr], gp.at[0, c, zh, y]
    far_g = send(mine_g, mine_g, zh_peer)
    far_w = send(mine_w, mine_w, zq_peer)
    near = send_near(mine_g)
    cross = [send(mine_g, mine_g, core_peer)]
    plane = send_plane(mine_w)
    for load in loads[2:]:
        load.wait()
    for i in range(X):
        turned = raw[i].reshape(xbins, C * cframes).T
        for j in range(C * ZH * Y):
            spec_t[i, j % C, pl.ds(j // C * grows, grows)] = turned[j * grows:(j + 1) * grows]
    cross += wait_near(near, lambda y_: gp.at[0, c, zh, y_])
    far_w.wait_recv()
    there = wp.at[0, x, 1 - zq, zr]
    plane_far = send_plane(there)
    far_g.wait_recv()
    wait_all(cross)
    there = gp.at[0, c, 1 - zh, y]
    near = send_near(there)
    cross = [send(there, there, core_peer)]
    wait_all(plane.values())
    wait_all(plane_far.values())
    plane = None

    def acts_terms(it, c_, zh_, xs):
        w = halves(jnp.concatenate([wp[it, i].reshape(xbins, K) for i in xs], axis=0))
        if zh_ is None:
            g, rows = gp[it, c_].reshape(cframes, K), pl.ds(0, cframes)
        else:
            g, rows = gp[it, c_, zh_].reshape(Y * grows, K), pl.ds(zh_ * Y * grows, Y * grows)
        s = jnp.concatenate([spec_t[i, c_, rows] for i in xs], axis=1)
        return rows, inner(halves(s / outer(halves(g), w)), w)

    def basis_terms(it, xs, c_):
        w = halves(jnp.concatenate([wp[it, i].reshape(xbins, K) for i in xs], axis=0))
        g = halves(gp[it + 1, c_].reshape(cframes, K))
        s = jnp.concatenate([spec[c_, i] for i in xs], axis=0)
        return inner(halves(s / outer(w, g)), g)

    for it in range(ITERS):
        def add_terms(c_, zh_, xs, fresh):
            rows, terms = acts_terms(it, c_, zh_, xs)
            fcore[it, c_, rows] = terms if fresh else fcore[it, c_, rows] + terms

        sides = [(1 - c, zh), (c, zh), (1 - c, 1 - zh), (c, 1 - zh)]
        others = [step(x, d, X) for d in (1, 3, 2)]
        if it == 0:
            for side in sides[:2]:
                add_terms(*side, [x, *others], True)
            cross += wait_near(near, lambda y_: gp.at[0, c, 1 - zh, y_])
            wait_all(cross)
        else:
            wait_all(plane[0, e] for e in range(1, ZR))
            for c_ in (1 - c, c):
                add_terms(c_, None, [x], True)
            wait_all(plane[at] for at in steps if at[0])
        sums = fold8(wp[it])
        for c_ in range(C):
            fcore[it, c_, pl.ds(cframes, 8)] = sums
        for i in range(C):
            if it:
                add_terms(sides[i][0], None, others, False)
            else:
                add_terms(*sides[2 + i], [x, *others], True)
            if i == 0:
                first = send(fcore.at[it, 1 - c], fcore_in.at[it], core_peer)
        first.wait_recv()
        total = fcore[it, c] + fcore_in[it]
        for i in range(Y):
            for j in range(ZH):
                at = (j * Y + i) * grows
                fy[it, i, pl.ds(j * grows, grows)] = total[at:at + grows]
            fy[it, i, pl.ds(gpart, 8)] = total[cframes:]
        near = {d: send(fy.at[it, step(y, d, Y)], fy_in.at[it, d - 1], y_peer[d]) for d in (2, 1, 3)}
        total = fy[it, y]
        for d in (1, 3, 2):
            near[d].wait_recv()
            total = total + fy_in[it, d - 1]
        fz[it] = total
        far = send(fz.at[it], fz_in.at[it], zh_peer)
        drain()
        if it == 0:
            for i in range(X):
                for j in range(C):
                    spec[j, i] = spec_t[i, j].T
        far.wait_recv()
        total = total + fz_in[it]
        scale = jnp.sum(total[gpart:], axis=0)
        gp[it + 1, c, :, y] = gp[it, c, :, y] * total[:gpart].reshape(ZH, grows, K) / scale
        mine = gp.at[it + 1, c, :, y]
        near = send_near(mine)
        cross = [send(mine, mine, core_peer)]
        if it + 1 == ITERS:
            acts_out[...] = gp[it + 1, c, zh, y]
        cross += wait_near(near, lambda y_: gp.at[it + 1, c, :, y_])

        for i in range(0, X, GROUP):
            terms = basis_terms(it, range(i, i + GROUP), c)
            for j in range(GROUP):
                wacc[i + j] = terms[j * xbins:(j + 1) * xbins]
        sums = fold8(gp[it + 1, c])
        wait_all(cross)
        sums = sums + fold8(gp[it + 1, 1 - c])
        rs[it] = sums
        totals = {at: send(rs.at[it], rs_in.at[it, at[0], at[1]], xz_peer[at]) for at in steps}
        plane = {}
        for ds in PAIRS:
            xs = [step(x, d, X) for d in ds]
            both = basis_terms(it, xs, 1 - c)
            for n, x_ in enumerate(xs):
                terms = wacc[x_] + both[n * xbins:(n + 1) * xbins]
                for i in range(ZR):
                    for j in range(ZQ):
                        at = (j * ZR + i) * wrows
                        rx[it, x_, i, pl.ds(j * wrows, wrows)] = terms[at:at + wrows]
                for at in steps:
                    if at[0] == ds[n]:
                        src = rx.at[it, x_, step(zr, at[1], ZR)]
                        plane[at] = send(src, rx_in.at[it, at[0], at[1]], xz_peer[at])
        for at in steps:
            totals[at].wait_recv()
            sums = sums + rs_in[it, at[0], at[1]]
        total = rx[it, x, zr]
        for at in sorted(steps):
            plane[at].wait_recv()
            total = total + rx_in[it, at[0], at[1]]
        rq[it, pl.ds(0, wpart)] = total
        rq[it, pl.ds(wpart, 8)] = sums
        far = send(rq.at[it], rq_in.at[it], zq_peer)
        drain()
        far.wait_recv()
        total = (total + rq_in[it, pl.ds(0, wpart)]).reshape(ZQ, wrows, K)
        scale = jnp.sum(sums + rq_in[it, pl.ds(wpart, 8)], axis=0)
        wp[it + 1, x, :, zr] = wp[it, x, :, zr] * total / scale
        if it + 1 < ITERS:
            plane = send_plane(wp.at[it + 1, x, :, zr])
        else:
            basis_out[...] = wp[it + 1, x, zq, zr]

    for copy in copies[len(drained):]:
        copy.wait_send()


def per_device(spectrum, basis, activations):
    bins, frames = spectrum.shape
    wrows, grows = basis.shape[0], activations.shape[0]
    gpart, wpart = ZH * grows, ZQ * wrows
    fwide = Y * gpart + 8
    anywhere = pl.BlockSpec(memory_space=pl.ANY)
    vmem = pl.BlockSpec(memory_space=pltpu.VMEM)
    return pl.pallas_call(
        kernel,
        out_shape=(
            pltpu.VMEM(basis.shape, F32),
            pltpu.VMEM(activations.shape, F32),
        ),
        in_specs=[anywhere] * 3,
        out_specs=(vmem, vmem),
        scratch_shapes=[
            pltpu.VMEM((X, ZQ * ZR, wrows, frames), F32),
            pltpu.VMEM((C, X, bins // X, frames // C), F32),
            pltpu.VMEM((X, C, frames // C, bins // X), F32),
            pltpu.VMEM((ITERS + 1, X, ZQ, ZR, wrows, K), F32),
            pltpu.VMEM((ITERS + 1, C, ZH, Y, grows, K), F32),
            pltpu.VMEM((ITERS, C, fwide, K), F32),
            pltpu.VMEM((ITERS, fwide, K), F32),
            pltpu.VMEM((ITERS, Y, gpart + 8, K), F32),
            pltpu.VMEM((ITERS, Y - 1, gpart + 8, K), F32),
            pltpu.VMEM((ITERS, gpart + 8, K), F32),
            pltpu.VMEM((ITERS, gpart + 8, K), F32),
            pltpu.VMEM((X, bins // X, K), F32),
            pltpu.VMEM((ITERS, X, ZR, wpart, K), F32),
            pltpu.VMEM((ITERS, X, ZR, wpart, K), F32),
            pltpu.VMEM((ITERS, 8, K), F32),
            pltpu.VMEM((ITERS, X, ZR, 8, K), F32),
            pltpu.VMEM((ITERS, wpart + 8, K), F32),
            pltpu.VMEM((ITERS, wpart + 8, K), F32),
            pltpu.SemaphoreType.DMA((2 + X,)),
            pltpu.SemaphoreType.DMA((SEMS,)),
            pltpu.SemaphoreType.DMA((SEMS,)),
        ],
        compiler_params=pltpu.CompilerParams(
            collective_id=0, has_side_effects=True, vmem_limit_bytes=62914560
        ),
    )(spectrum.reshape(ZQ * ZR, X, wrows, frames), basis, activations)


def solution(mesh):
    return jax.shard_map(
        per_device,
        mesh=mesh,
        in_specs=(P("freq", "frame"), P(("freq", "frame"), None), P(("frame", "freq"), None)),
        out_specs=(P(("freq", "frame"), None), P(("frame", "freq"), None)),
        check_vma=False,
    )
```

```python
import jax
import jax.numpy as jnp
from jax import lax
from jax.experimental import pallas as pl
from jax.experimental.pallas import tpu as pltpu
from jax.sharding import PartitionSpec as P

ITERS = 2
K = 128
X, ZR, ZQ = 4, 4, 2
Y, ZH, C = 4, 2, 2
SEMS = 192
GROUP = 2
PAIRS = ((2, 1), (3, 0))
F32, BF16 = jnp.float32, jnp.bfloat16


def halves(value):
    high = value.astype(BF16)
    return high, (value - high.astype(F32)).astype(BF16)


def dot(left, right, contract_right):
    return lax.dot_general(
        left, right, (((1,), (contract_right,)), ((), ())), preferred_element_type=F32
    )


def outer(left, right):
    wide = dot(jnp.concatenate(left, axis=1), jnp.concatenate([right[0], right[0]], axis=1), 1)
    return wide + dot(left[0], right[1], 1)


def inner(left, right):
    wide = dot(left[0], jnp.concatenate(right, axis=1), 0)
    return wide[:, :K] + wide[:, K:] + dot(left[1], right[0], 0)


def fold8(value):
    return jnp.sum(value.reshape(-1, 8, K), axis=0)


def kernel(
    spec_hbm, basis_hbm, acts_hbm, basis_out, acts_out,
    raw, spec, spec_t, wp, gp,
    fcore, fcore_in, fy, fy_in, fz, fz_in,
    wacc, rx, rx_in, rs, rs_in, rq, rq_in, ex, ex_in, ez, ez_in,
    load_sem, send_sem, recv_sem,
):
    fr = lax.axis_index("frame")
    fq = lax.axis_index("freq")
    x, zl = lax.rem(fr, X), lax.div(fr, X)
    zr, zq = lax.rem(zl, ZR), lax.div(zl, ZR)
    c, yz = lax.rem(fq, C), lax.div(fq, C)
    y, zh = lax.rem(yz, Y), lax.div(yz, Y)
    wrows, grows = basis_hbm.shape[0], acts_hbm.shape[0]
    xbins, cframes = ZQ * ZR * wrows, ZH * Y * grows
    wpart = ZQ * wrows

    def frame_at(zq_, zr_, x_):
        return ((zq_ * ZR + zr_) * X + x_, fq)

    def freq_at(zh_, y_, c_):
        return (fr, (zh_ * Y + y_) * C + c_)

    def step(value, by, size):
        return lax.rem(value + by, size)

    core_peer = freq_at(zh, y, 1 - c)
    zh_peer = freq_at(1 - zh, y, c)
    zq_peer = frame_at(1 - zq, zr, x)
    y_peer = {d: freq_at(zh, step(y, d, Y), c) for d in (2, 1, 3)}
    steps = [(d, e) for d in (2, 1, 3, 0) for e in (2, 1, 3, 0) if d or e]
    xz_peer = {(d, e): frame_at(zq, step(zr, e, ZR), step(x, d, X)) for d, e in steps}
    peers = [zh_peer, zq_peer, *xz_peer.values(), *y_peer.values(), core_peer]

    barrier = pltpu.get_barrier_semaphore()
    for peer in peers:
        pl.semaphore_signal(barrier, inc=1, device_id=peer, device_id_type=pl.DeviceIdType.MESH)

    loads = [
        pltpu.make_async_copy(acts_hbm, gp.at[0, c, zh, y], load_sem.at[0]),
        pltpu.make_async_copy(basis_hbm, wp.at[0, x, zq, zr], load_sem.at[1]),
    ]
    for i in range(X):
        loads.append(pltpu.make_async_copy(spec_hbm.at[:, i], raw.at[i], load_sem.at[2 + i]))
    for load in loads:
        load.start()
    loads[0].wait()
    loads[1].wait()
    pl.semaphore_wait(barrier, len(peers))

    copies, drained = [], []

    def drain(last):
        for copy in copies[len(drained):-last]:
            copy.wait_send()
            drained.append(copy)

    def send(src, dst, peer):
        slot = len(copies)
        copy = pltpu.make_async_remote_copy(
            src_ref=src, dst_ref=dst, send_sem=send_sem.at[slot], recv_sem=recv_sem.at[slot],
            device_id=peer, device_id_type=pl.DeviceIdType.MESH,
        )
        copy.start()
        copies.append(copy)
        return copy

    def send_near(ref):
        return {d: send(ref, ref, y_peer[d]) for d in (2, 1, 3)}

    def send_plane(ref):
        return {at: send(ref, ref, xz_peer[at]) for at in steps}

    def wait_all(waits):
        for wait in waits:
            wait.wait_recv()

    def wait_near(near, part):
        passed = []
        for d in (1, 3, 2):
            near[d].wait_recv()
            there = part(step(y, Y - d, Y))
            passed.append(send(there, there, core_peer))
        return passed

    mine_w, mine_g = wp.at[0, x, zq, zr], gp.at[0, c, zh, y]
    far_g = send(mine_g, mine_g, zh_peer)
    far_w = send(mine_w, mine_w, zq_peer)
    near = send_near(mine_g)
    cross = [send(mine_g, mine_g, core_peer)]
    plane = send_plane(mine_w)
    for load in loads[2:]:
        load.wait()
    for i in range(X):
        turned = raw[i].reshape(xbins, C * cframes).T
        for j in range(C * ZH * Y):
            spec_t[i, j % C, pl.ds(j // C * grows, grows)] = turned[j * grows:(j + 1) * grows]
    cross += wait_near(near, lambda y_: gp.at[0, c, zh, y_])
    far_w.wait_recv()
    there = wp.at[0, x, 1 - zq, zr]
    plane_far = send_plane(there)
    far_g.wait_recv()
    wait_all(cross)
    there = gp.at[0, c, 1 - zh, y]
    far_near = send_near(there)
    cross = [send(there, there, core_peer)]
    wait_all(plane.values())
    wait_all(plane_far.values())
    plane = None

    def acts_terms(it, c_, zh_, xs):
        w = halves(jnp.concatenate([wp[it, i].reshape(xbins, K) for i in xs], axis=0))
        if zh_ is None:
            g, rows = gp[it, c_].reshape(cframes, K), pl.ds(0, cframes)
        else:
            g, rows = gp[it, c_, zh_].reshape(Y * grows, K), pl.ds(zh_ * Y * grows, Y * grows)
        s = jnp.concatenate([spec_t[i, c_, rows] for i in xs], axis=1)
        return inner(halves(s / outer(halves(g), w)), w)

    def basis_terms(it, xs, c_):
        w = halves(jnp.concatenate([wp[it, i].reshape(xbins, K) for i in xs], axis=0))
        g = halves(gp[it + 1, c_].reshape(cframes, K))
        s = jnp.concatenate([spec[c_, i] for i in xs], axis=0)
        return inner(halves(s / outer(w, g)), g)

    half, tail = Y * grows, pl.ds(grows, 8)

    for it in range(ITERS):
        order = (0, 1) if it else (zh, 1 - zh)
        arrival = (0, 1) if it else (1 - zh, zh)
        others = [step(x, d, X) for d in (1, 3, 2)]

        def add_terms(c_, k, xs):
            terms = acts_terms(it, c_, order[k], xs)
            rows = pl.ds(0, half)
            fcore[it, c_, order[k], rows] = fcore[it, c_, order[k], rows] + terms if it else terms

        def send_core(k):
            rows = pl.ds(0, half if k else half + 8)
            return send(fcore.at[it, 1 - c, order[k], rows], fcore_in.at[it, order[k], rows], core_peer)

        def send_y(k, core):
            h, n = order[k], grows if k else grows + 8
            core.wait_recv()
            for i in range(Y):
                rows = pl.ds(i * grows, grows)
                fy[it, h, i, pl.ds(0, grows)] = fcore[it, c, h, rows] + fcore_in[it, h, rows]
                if k == 0:
                    rows = pl.ds(half, 8)
                    fy[it, h, i, tail] = fcore[it, c, h, rows] + fcore_in[it, h, rows]
            rows = pl.ds(0, n)
            return {
                d: send(fy.at[it, h, step(y, d, Y), rows], fy_in.at[it, h, d - 1, rows], y_peer[d])
                for d in (2, 1, 3)
            }

        def send_far(k, near):
            h, rows = order[k], pl.ds(0, grows if k else grows + 8)
            total = fy[it, h, y, rows]
            for d in (1, 3, 2):
                near[d].wait_recv()
                total = total + fy_in[it, h, d - 1, rows]
            fz[it, h, rows] = total
            return send(fz.at[it, h, rows], fz_in.at[it, h, rows], zh_peer)

        if it:
            wait_all(plane[0, e] for e in range(1, ZR))
            for c_ in (1 - c, c):
                terms = acts_terms(it, c_, None, [x])
                for i in range(ZH):
                    fcore[it, c_, i, pl.ds(0, half)] = terms[i * half:(i + 1) * half]
            wait_all(plane[at] for at in steps if at[0])
        sums = fold8(wp[it])
        for c_ in range(C):
            fcore[it, c_, order[0], pl.ds(half, 8)] = sums
        xs = others if it else [x, *others]
        add_terms(1 - c, 0, xs)
        core = [send_core(0)]
        add_terms(c, 0, xs)
        if it:
            add_terms(1 - c, 1, xs)
            core.append(send_core(1))
            near = [send_y(0, core[0])]
            add_terms(c, 1, xs)
        else:
            cross += wait_near(far_near, lambda y_: gp.at[0, c, 1 - zh, y_])
            near = [send_y(0, core[0])]
            wait_all(cross)
            add_terms(1 - c, 1, xs)
            core.append(send_core(1))
            add_terms(c, 1, xs)
        near.append(send_y(1, core[1]))
        far = [send_far(k, near[k]) for k in range(ZH)]
        drain(ZH)
        if it == 0:
            for i in range(X):
                for j in range(C):
                    spec[j, i] = spec_t[i, j].T
        near, cross = [], []
        for k in range(ZH):
            far[k].wait_recv()
            h = arrival[k]
            if k == 0:
                scale = jnp.sum(fz[it, order[0], tail] + fz_in[it, h, tail], axis=0)
            rows = pl.ds(0, grows)
            gp[it + 1, c, h, y] = gp[it, c, h, y] * (fz[it, h, rows] + fz_in[it, h, rows]) / scale
            mine = gp.at[it + 1, c, h, y]
            near.append(send_near(mine))
            cross.append(send(mine, mine, core_peer))
        if it + 1 == ITERS:
            acts_out[...] = gp[it + 1, c, zh, y]
        for k in range(ZH):
            cross += wait_near(near[k], lambda y_: gp.at[it + 1, c, arrival[k], y_])

        for i in range(0, X, GROUP):
            terms = basis_terms(it, range(i, i + GROUP), c)
            for j in range(GROUP):
                wacc[i + j] = terms[j * xbins:(j + 1) * xbins]
        sums = fold8(gp[it + 1, c])
        wait_all(cross)
        sums = sums + fold8(gp[it + 1, 1 - c])
        rs[it] = sums
        totals = {at: send(rs.at[it], rs_in.at[it, at[0], at[1]], xz_peer[at]) for at in steps}
        plane = {}
        for ds in PAIRS:
            xs = [step(x, d, X) for d in ds]
            both = basis_terms(it, xs, 1 - c)
            for n, x_ in enumerate(xs):
                terms = wacc[x_] + both[n * xbins:(n + 1) * xbins]
                if it + 1 == ITERS:
                    ex[x_] = terms
                    if ds[n]:
                        plane[ds[n]] = send(ex.at[x_], ex_in.at[ds[n] - 1], xz_peer[ds[n], 0])
                    continue
                for i in range(ZR):
                    for j in range(ZQ):
                        at = (j * ZR + i) * wrows
                        rx[x_, i, pl.ds(j * wrows, wrows)] = terms[at:at + wrows]
                for at in steps:
                    if at[0] == ds[n]:
                        src = rx.at[x_, step(zr, at[1], ZR)]
                        plane[at] = send(src, rx_in.at[at[0], at[1]], xz_peer[at])
        for at in steps:
            totals[at].wait_recv()
            sums = sums + rs_in[it, at[0], at[1]]
        rq[it, pl.ds(wpart, 8)] = sums
        if it + 1 == ITERS:
            rows = pl.ds(wpart, 8)
            far = send(rq.at[it, rows], rq_in.at[it, rows], zq_peer)
            total = ex[x]
            for d in (1, 3, 2):
                plane[d].wait_recv()
                total = total + ex_in[d - 1]
            ez[...] = total.reshape(ZQ * ZR, wrows, K)
            parts = {}
            for d in (4, 3, 5, 2, 6, 1, 7):
                there = step(zl, d, ZQ * ZR)
                parts[d] = send(ez.at[there], ez_in.at[d - 1], (there * X + x, fq))
            drain(ZQ * ZR)
            far.wait_recv()
            scale = jnp.sum(sums + rq_in[it, rows], axis=0)
            total = ez[zl]
            for d in (1, 7, 2, 6, 3, 5, 4):
                parts[d].wait_recv()
                total = total + ez_in[d - 1]
            basis_out[...] = wp[it, x, zq, zr] * total / scale
            continue
        total = rx[x, zr]
        for at in sorted(steps):
            plane[at].wait_recv()
            total = total + rx_in[at[0], at[1]]
        rq[it, pl.ds(0, wpart)] = total
        far = send(rq.at[it], rq_in.at[it], zq_peer)
        drain(1)
        far.wait_recv()
        total = (total + rq_in[it, pl.ds(0, wpart)]).reshape(ZQ, wrows, K)
        scale = jnp.sum(sums + rq_in[it, pl.ds(wpart, 8)], axis=0)
        wp[it + 1, x, :, zr] = wp[it, x, :, zr] * total / scale
        plane = send_plane(wp.at[it + 1, x, :, zr])

    for copy in copies[len(drained):]:
        copy.wait_send()


def per_device(spectrum, basis, activations):
    bins, frames = spectrum.shape
    wrows, grows = basis.shape[0], activations.shape[0]
    wpart = ZQ * wrows
    anywhere = pl.BlockSpec(memory_space=pl.ANY)
    vmem = pl.BlockSpec(memory_space=pltpu.VMEM)
    return pl.pallas_call(
        kernel,
        out_shape=(
            pltpu.VMEM(basis.shape, F32),
            pltpu.VMEM(activations.shape, F32),
        ),
        in_specs=[anywhere] * 3,
        out_specs=(vmem, vmem),
        scratch_shapes=[
            pltpu.VMEM((X, ZQ * ZR, wrows, frames), F32),
            pltpu.VMEM((C, X, bins // X, frames // C), F32),
            pltpu.VMEM((X, C, frames // C, bins // X), F32),
            pltpu.VMEM((ITERS + 1, X, ZQ, ZR, wrows, K), F32),
            pltpu.VMEM((ITERS + 1, C, ZH, Y, grows, K), F32),
            pltpu.VMEM((ITERS, C, ZH, Y * grows + 8, K), F32),
            pltpu.VMEM((ITERS, ZH, Y * grows + 8, K), F32),
            pltpu.VMEM((ITERS, ZH, Y, grows + 8, K), F32),
            pltpu.VMEM((ITERS, ZH, Y - 1, grows + 8, K), F32),
            pltpu.VMEM((ITERS, ZH, grows + 8, K), F32),
            pltpu.VMEM((ITERS, ZH, grows + 8, K), F32),
            pltpu.VMEM((X, bins // X, K), F32),
            pltpu.VMEM((X, ZR, wpart, K), F32),
            pltpu.VMEM((X, ZR, wpart, K), F32),
            pltpu.VMEM((ITERS, 8, K), F32),
            pltpu.VMEM((ITERS, X, ZR, 8, K), F32),
            pltpu.VMEM((ITERS, wpart + 8, K), F32),
            pltpu.VMEM((ITERS, wpart + 8, K), F32),
            pltpu.VMEM((X, bins // X, K), F32),
            pltpu.VMEM((X - 1, bins // X, K), F32),
            pltpu.VMEM((ZQ * ZR, wrows, K), F32),
            pltpu.VMEM((ZQ * ZR - 1, wrows, K), F32),
            pltpu.SemaphoreType.DMA((2 + X,)),
            pltpu.SemaphoreType.DMA((SEMS,)),
            pltpu.SemaphoreType.DMA((SEMS,)),
        ],
        compiler_params=pltpu.CompilerParams(
            collective_id=0, has_side_effects=True, vmem_limit_bytes=62914560
        ),
    )(spectrum.reshape(ZQ * ZR, X, wrows, frames), basis, activations)


def solution(mesh):
    return jax.shard_map(
        per_device,
        mesh=mesh,
        in_specs=(P("freq", "frame"), P(("freq", "frame"), None), P(("frame", "freq"), None)),
        out_specs=(P(("freq", "frame"), None), P(("frame", "freq"), None)),
        check_vma=False,
    )
```

```python
import jax
import jax.numpy as jnp
from jax import lax
from jax.experimental import pallas as pl
from jax.experimental.pallas import tpu as pltpu
from jax.sharding import PartitionSpec as P

ITERS = 2
K = 128
X, ZR, ZQ = 4, 4, 2
Y, ZH, C = 4, 2, 2
SEMS = 224
GROUP = 2
PAIRS = ((2, 1), (3, 0))
F32, BF16 = jnp.float32, jnp.bfloat16


def halves(value):
    high = value.astype(BF16)
    return high, (value - high.astype(F32)).astype(BF16)


def dot(left, right, contract_right):
    return lax.dot_general(
        left, right, (((1,), (contract_right,)), ((), ())), preferred_element_type=F32
    )


def outer(left, right):
    wide = dot(jnp.concatenate(left, axis=1), jnp.concatenate([right[0], right[0]], axis=1), 1)
    return wide + dot(left[0], right[1], 1)


def inner(left, right):
    wide = dot(left[0], jnp.concatenate(right, axis=1), 0)
    return wide[:, :K] + wide[:, K:] + dot(left[1], right[0], 0)


def fold8(value):
    return jnp.sum(value.reshape(-1, 8, K), axis=0)


def kernel(
    spec_hbm, basis_hbm, acts_hbm, basis_out, acts_out,
    raw, spec, spec_t, wp, gp,
    fcore, fcore_in, fy, fy_in, fz, fz_in,
    wacc, rx, rx_in, rt, rs, rs_in, rq, rq_in, ex_in, ez, ez_in,
    load_sem, send_sem, recv_sem,
):
    fr = lax.axis_index("frame")
    fq = lax.axis_index("freq")
    x, zl = lax.rem(fr, X), lax.div(fr, X)
    zr, zq = lax.rem(zl, ZR), lax.div(zl, ZR)
    c, yz = lax.rem(fq, C), lax.div(fq, C)
    y, zh = lax.rem(yz, Y), lax.div(yz, Y)
    wrows, grows = basis_hbm.shape[0], acts_hbm.shape[0]
    xbins, cframes = ZQ * ZR * wrows, ZH * Y * grows

    def frame_at(zq_, zr_, x_):
        return ((zq_ * ZR + zr_) * X + x_, fq)

    def freq_at(zh_, y_, c_):
        return (fr, (zh_ * Y + y_) * C + c_)

    def step(value, by, size):
        return lax.rem(value + by, size)

    core_peer = freq_at(zh, y, 1 - c)
    zh_peer = freq_at(1 - zh, y, c)
    zq_peer = frame_at(1 - zq, zr, x)
    y_peer = {d: freq_at(zh, step(y, d, Y), c) for d in (2, 1, 3)}
    steps = [(d, e) for d in (2, 1, 3, 0) for e in (2, 1, 3, 0) if d or e]
    xz_peer = {(d, e): frame_at(zq, step(zr, e, ZR), step(x, d, X)) for d, e in steps}
    peers = [zh_peer, zq_peer, *xz_peer.values(), *y_peer.values(), core_peer]

    barrier = pltpu.get_barrier_semaphore()
    for peer in peers:
        pl.semaphore_signal(barrier, inc=1, device_id=peer, device_id_type=pl.DeviceIdType.MESH)

    loads = [
        pltpu.make_async_copy(acts_hbm, gp.at[0, c, zh, y], load_sem.at[0]),
        pltpu.make_async_copy(basis_hbm, wp.at[0, x, zq, zr], load_sem.at[1]),
    ]
    for i in range(X):
        loads.append(pltpu.make_async_copy(spec_hbm.at[:, i], raw.at[i], load_sem.at[2 + i]))
    for load in loads:
        load.start()
    loads[0].wait()
    loads[1].wait()
    pl.semaphore_wait(barrier, len(peers))

    copies, drained = [], []

    def drain(last):
        for copy in copies[len(drained):-last]:
            copy.wait_send()
            drained.append(copy)

    def send(src, dst, peer):
        slot = len(copies)
        copy = pltpu.make_async_remote_copy(
            src_ref=src, dst_ref=dst, send_sem=send_sem.at[slot], recv_sem=recv_sem.at[slot],
            device_id=peer, device_id_type=pl.DeviceIdType.MESH,
        )
        copy.start()
        copies.append(copy)
        return copy

    def send_near(ref):
        return {d: send(ref, ref, y_peer[d]) for d in (2, 1, 3)}

    def send_plane(ref):
        return {at: send(ref, ref, xz_peer[at]) for at in steps}

    def wait_all(waits):
        for wait in waits:
            wait.wait_recv()

    def wait_near(near, part):
        passed = []
        for d in (1, 3, 2):
            near[d].wait_recv()
            there = part(step(y, Y - d, Y))
            passed.append(send(there, there, core_peer))
        return passed

    mine_w, mine_g = wp.at[0, x, zq, zr], gp.at[0, c, zh, y]
    far_g = send(mine_g, mine_g, zh_peer)
    far_w = send(mine_w, mine_w, zq_peer)
    near = send_near(mine_g)
    cross = [send(mine_g, mine_g, core_peer)]
    plane = send_plane(mine_w)
    for load in loads[2:]:
        load.wait()
    for i in range(X):
        turned = raw[i].reshape(xbins, C * cframes).T
        for j in range(C * ZH * Y):
            spec_t[i, j % C, pl.ds(j // C * grows, grows)] = turned[j * grows:(j + 1) * grows]
    cross += wait_near(near, lambda y_: gp.at[0, c, zh, y_])
    far_w.wait_recv()
    there = wp.at[0, x, 1 - zq, zr]
    plane_far = send_plane(there)
    far_g.wait_recv()
    wait_all(cross)
    there = gp.at[0, c, 1 - zh, y]
    far_near = send_near(there)
    cross = [send(there, there, core_peer)]
    wait_all(plane.values())
    wait_all(plane_far.values())
    plane = None

    def acts_terms(it, c_, zh_, xs):
        w = halves(jnp.concatenate([wp[it, i].reshape(xbins, K) for i in xs], axis=0))
        if zh_ is None:
            g, rows = gp[it, c_].reshape(cframes, K), pl.ds(0, cframes)
        else:
            g, rows = gp[it, c_, zh_].reshape(Y * grows, K), pl.ds(zh_ * Y * grows, Y * grows)
        s = jnp.concatenate([spec_t[i, c_, rows] for i in xs], axis=1)
        return inner(halves(s / outer(halves(g), w)), w)

    def basis_terms(it, xs, c_):
        w = halves(jnp.concatenate([wp[it, i].reshape(xbins, K) for i in xs], axis=0))
        g = halves(gp[it + 1, c_].reshape(cframes, K))
        s = jnp.concatenate([spec[c_, i] for i in xs], axis=0)
        return inner(halves(s / outer(w, g)), g)

    half, tail = Y * grows, pl.ds(grows, 8)

    for it in range(ITERS):
        order = (0, 1) if it else (zh, 1 - zh)
        arrival = (0, 1) if it else (1 - zh, zh)
        others = [step(x, d, X) for d in (1, 3, 2)]

        def add_terms(c_, k, xs):
            terms = acts_terms(it, c_, order[k], xs)
            rows = pl.ds(0, half)
            fcore[it, c_, order[k], rows] = fcore[it, c_, order[k], rows] + terms if it else terms

        def send_core(k):
            rows = pl.ds(0, half if k else half + 8)
            return send(fcore.at[it, 1 - c, order[k], rows], fcore_in.at[it, order[k], rows], core_peer)

        def send_y(k, core):
            h, n = order[k], grows if k else grows + 8
            core.wait_recv()
            for i in range(Y):
                rows = pl.ds(i * grows, grows)
                fy[it, h, i, pl.ds(0, grows)] = fcore[it, c, h, rows] + fcore_in[it, h, rows]
                if k == 0:
                    rows = pl.ds(half, 8)
                    fy[it, h, i, tail] = fcore[it, c, h, rows] + fcore_in[it, h, rows]
            rows = pl.ds(0, n)
            return {
                d: send(fy.at[it, h, step(y, d, Y), rows], fy_in.at[it, h, d - 1, rows], y_peer[d])
                for d in (2, 1, 3)
            }

        def send_far(k, near):
            h, rows = order[k], pl.ds(0, grows if k else grows + 8)
            total = fy[it, h, y, rows]
            for d in (1, 3, 2):
                near[d].wait_recv()
                total = total + fy_in[it, h, d - 1, rows]
            fz[it, h, rows] = total
            return send(fz.at[it, h, rows], fz_in.at[it, h, rows], zh_peer)

        if it:
            wait_all(part[0, e] for part in plane_parts for e in range(1, ZR))
            for c_ in (1 - c, c):
                terms = acts_terms(it, c_, None, [x])
                for i in range(ZH):
                    fcore[it, c_, i, pl.ds(0, half)] = terms[i * half:(i + 1) * half]
            wait_all(part[at] for part in plane_parts for at in steps if at[0])
        sums = fold8(wp[it])
        for c_ in range(C):
            fcore[it, c_, order[0], pl.ds(half, 8)] = sums
        xs = others if it else [x, *others]
        add_terms(1 - c, 0, xs)
        core = [send_core(0)]
        if it:
            add_terms(1 - c, 1, xs)
            core.append(send_core(1))
            add_terms(c, 0, xs)
            near = [send_y(0, core[0])]
            add_terms(c, 1, xs)
        else:
            add_terms(c, 0, xs)
            cross += wait_near(far_near, lambda y_: gp.at[0, c, 1 - zh, y_])
            near = [send_y(0, core[0])]
            add_terms(c, 1, xs)
            wait_all(cross)
            add_terms(1 - c, 1, xs)
            core.append(send_core(1))
        near.append(send_y(1, core[1]))
        far = [send_far(k, near[k]) for k in range(ZH)]
        drain(ZH)
        if it == 0:
            for i in range(X):
                for j in range(C):
                    spec[j, i] = spec_t[i, j].T
        near, cross = [], []
        for k in range(ZH):
            far[k].wait_recv()
            h = arrival[k]
            if k == 0:
                scale = jnp.sum(fz[it, order[0], tail] + fz_in[it, h, tail], axis=0)
            rows = pl.ds(0, grows)
            gp[it + 1, c, h, y] = gp[it, c, h, y] * (fz[it, h, rows] + fz_in[it, h, rows]) / scale
            mine = gp.at[it + 1, c, h, y]
            near.append(send_near(mine))
            cross.append(send(mine, mine, core_peer))
        if it + 1 == ITERS:
            acts_out[...] = gp[it + 1, c, zh, y]
        for k in range(ZH):
            cross += wait_near(near[k], lambda y_: gp.at[it + 1, c, arrival[k], y_])

        for i in range(0, X, GROUP):
            terms = basis_terms(it, range(i, i + GROUP), c)
            for j in range(GROUP):
                wacc[i + j] = terms[j * xbins:(j + 1) * xbins]
        sums = fold8(gp[it + 1, c])
        wait_all(cross)
        sums = sums + fold8(gp[it + 1, 1 - c])
        rt[it] = sums
        totals = {at: send(rt.at[it], rs_in.at[it, at[0], at[1]], xz_peer[at]) for at in steps}
        plane = {}
        sides = (1 - zq, zq) if it + 1 == ITERS else range(ZQ)
        for ds in PAIRS:
            xs = [step(x, d, X) for d in ds]
            both = basis_terms(it, xs, 1 - c)
            for n, x_ in enumerate(xs):
                terms = wacc[x_] + both[n * xbins:(n + 1) * xbins]
                rx[it, x_] = terms.reshape(ZQ, ZR, wrows, K)
            for k, j in enumerate(sides):
                for d, x_ in zip(ds, xs):
                    if it + 1 < ITERS:
                        for at in steps:
                            if at[0] == d:
                                src = rx.at[it, x_, j, step(zr, at[1], ZR)]
                                plane[k, at] = send(src, rx_in.at[at[0], j, at[1]], xz_peer[at])
                    elif d:
                        plane[k, d] = send(rx.at[it, x_, j], ex_in.at[d - 1, j], xz_peer[d, 0])
        for at in steps:
            totals[at].wait_recv()
            sums = sums + rs_in[it, at[0], at[1]]
        rs[it] = sums
        swap = send(rs.at[it], rs_in.at[it, 0, 0], zq_peer)
        if it + 1 < ITERS:
            far = []
            for j in range(ZQ):
                total = rx[it, x, j, zr]
                for at in sorted(steps):
                    plane[j, at].wait_recv()
                    total = total + rx_in[at[0], j, at[1]]
                rq[j] = total
                far.append(send(rq.at[j], rq_in.at[j], zq_peer))
            drain(1 + ZQ)
            swap.wait_recv()
            scale = jnp.sum(sums + rs_in[it, 0, 0], axis=0)
            plane_parts = []
            for j in range(ZQ):
                far[j].wait_recv()
                wp[it + 1, x, j, zr] = wp[it, x, j, zr] * (rq[j] + rq_in[j]) / scale
                plane_parts.append(send_plane(wp.at[it + 1, x, j, zr]))
        else:
            parts = {}
            for k, j in enumerate(sides):
                total = rx[it, x, j]
                for d in (1, 3, 2):
                    plane[k, d].wait_recv()
                    total = total + ex_in[d - 1, j]
                ez[j] = total
                for e in (2, 1, 3, 0):
                    if e or k == 0:
                        there = step(zr, e, ZR)
                        parts[k, e] = send(ez.at[j, there], ez_in.at[k, e], frame_at(j, there, x))
            drain(ZQ * ZR)
            swap.wait_recv()
            scale = jnp.sum(sums + rs_in[it, 0, 0], axis=0)
            total = ez[zq, zr]
            for k in (1, 0):
                for e in (1, 3, 2, 0):
                    if e or k == 0:
                        parts[k, e].wait_recv()
                        total = total + ez_in[k, e]
            basis_out[...] = wp[it, x, zq, zr] * total / scale

    for copy in copies[len(drained):]:
        copy.wait_send()


def per_device(spectrum, basis, activations):
    bins, frames = spectrum.shape
    wrows, grows = basis.shape[0], activations.shape[0]
    anywhere = pl.BlockSpec(memory_space=pl.ANY)
    vmem = pl.BlockSpec(memory_space=pltpu.VMEM)
    return pl.pallas_call(
        kernel,
        out_shape=(
            pltpu.VMEM(basis.shape, F32),
            pltpu.VMEM(activations.shape, F32),
        ),
        in_specs=[anywhere] * 3,
        out_specs=(vmem, vmem),
        scratch_shapes=[
            pltpu.VMEM((X, ZQ * ZR, wrows, frames), F32),
            pltpu.VMEM((C, X, bins // X, frames // C), F32),
            pltpu.VMEM((X, C, frames // C, bins // X), F32),
            pltpu.VMEM((ITERS + 1, X, ZQ, ZR, wrows, K), F32),
            pltpu.VMEM((ITERS + 1, C, ZH, Y, grows, K), F32),
            pltpu.VMEM((ITERS, C, ZH, Y * grows + 8, K), F32),
            pltpu.VMEM((ITERS, ZH, Y * grows + 8, K), F32),
            pltpu.VMEM((ITERS, ZH, Y, grows + 8, K), F32),
            pltpu.VMEM((ITERS, ZH, Y - 1, grows + 8, K), F32),
            pltpu.VMEM((ITERS, ZH, grows + 8, K), F32),
            pltpu.VMEM((ITERS, ZH, grows + 8, K), F32),
            pltpu.VMEM((X, bins // X, K), F32),
            pltpu.VMEM((ITERS, X, ZQ, ZR, wrows, K), F32),
            pltpu.VMEM((X, ZQ, ZR, wrows, K), F32),
            pltpu.VMEM((ITERS, 8, K), F32),
            pltpu.VMEM((ITERS, 8, K), F32),
            pltpu.VMEM((ITERS, X, ZR, 8, K), F32),
            pltpu.VMEM((ZQ, wrows, K), F32),
            pltpu.VMEM((ZQ, wrows, K), F32),
            pltpu.VMEM((X - 1, ZQ, ZR, wrows, K), F32),
            pltpu.VMEM((ZQ, ZR, wrows, K), F32),
            pltpu.VMEM((ZQ, ZR, wrows, K), F32),
            pltpu.SemaphoreType.DMA((2 + X,)),
            pltpu.SemaphoreType.DMA((SEMS,)),
            pltpu.SemaphoreType.DMA((SEMS,)),
        ],
        compiler_params=pltpu.CompilerParams(
            collective_id=0, has_side_effects=True, vmem_limit_bytes=62914560
        ),
    )(spectrum.reshape(ZQ * ZR, X, wrows, frames), basis, activations)


def solution(mesh):
    return jax.shard_map(
        per_device,
        mesh=mesh,
        in_specs=(P("freq", "frame"), P(("freq", "frame"), None), P(("frame", "freq"), None)),
        out_specs=(P(("freq", "frame"), None), P(("frame", "freq"), None)),
        check_vma=False,
    )
```

```python
import jax
import jax.numpy as jnp
from jax import lax
from jax.experimental import pallas as pl
from jax.experimental.pallas import tpu as pltpu
from jax.sharding import PartitionSpec as P

ITERS = 2
K = 128
X, ZR, ZQ = 4, 4, 2
Y, ZH, C = 4, 2, 2
SEMS = 224
GROUP = 2
PAIRS = ((2, 1), (3, 0))
F32, BF16 = jnp.float32, jnp.bfloat16


def halves(value):
    high = value.astype(BF16)
    return high, (value - high.astype(F32)).astype(BF16)


def dot(left, right, contract_right):
    return lax.dot_general(
        left, right, (((1,), (contract_right,)), ((), ())), preferred_element_type=F32
    )


def outer(left, right):
    wide = dot(jnp.concatenate(left, axis=1), jnp.concatenate([right[0], right[0]], axis=1), 1)
    return wide + dot(left[0], right[1], 1)


def inner(left, right):
    wide = dot(left[0], jnp.concatenate(right, axis=1), 0)
    return wide[:, :K] + wide[:, K:] + dot(left[1], right[0], 0)


def fold8(value):
    return jnp.sum(value.reshape(-1, 8, K), axis=0)


def kernel(
    spec_hbm, basis_hbm, acts_hbm, basis_out, acts_out,
    raw, spec, spec_t, wp, gp,
    fcore, fcore_in, fy, fy_in, fz, fz_in,
    wacc, rx, rx_in, rt, rs, rs_in, rq, rq_in, ex_in, ez, ez_in,
    load_sem, send_sem, recv_sem,
):
    fr = lax.axis_index("frame")
    fq = lax.axis_index("freq")
    x, zl = lax.rem(fr, X), lax.div(fr, X)
    zr, zq = lax.rem(zl, ZR), lax.div(zl, ZR)
    c, yz = lax.rem(fq, C), lax.div(fq, C)
    y, zh = lax.rem(yz, Y), lax.div(yz, Y)
    wrows, grows = basis_hbm.shape[0], acts_hbm.shape[0]
    xbins, cframes = ZQ * ZR * wrows, ZH * Y * grows

    def frame_at(zq_, zr_, x_):
        return ((zq_ * ZR + zr_) * X + x_, fq)

    def freq_at(zh_, y_, c_):
        return (fr, (zh_ * Y + y_) * C + c_)

    def step(value, by, size):
        return lax.rem(value + by, size)

    core_peer = freq_at(zh, y, 1 - c)
    zh_peer = freq_at(1 - zh, y, c)
    zq_peer = frame_at(1 - zq, zr, x)
    y_peer = {d: freq_at(zh, step(y, d, Y), c) for d in (2, 1, 3)}
    steps = [(d, e) for d in (2, 1, 3, 0) for e in (2, 1, 3, 0) if d or e]
    xz_peer = {(d, e): frame_at(zq, step(zr, e, ZR), step(x, d, X)) for d, e in steps}
    peers = [zh_peer, zq_peer, *xz_peer.values(), *y_peer.values(), core_peer]

    barrier = pltpu.get_barrier_semaphore()
    for peer in peers:
        pl.semaphore_signal(barrier, inc=1, device_id=peer, device_id_type=pl.DeviceIdType.MESH)

    loads = [
        pltpu.make_async_copy(acts_hbm, gp.at[0, c, zh, y], load_sem.at[0]),
        pltpu.make_async_copy(basis_hbm, wp.at[0, x, zq, zr], load_sem.at[1]),
    ]
    for i in range(X):
        loads.append(pltpu.make_async_copy(spec_hbm.at[:, i], raw.at[i], load_sem.at[2 + i]))
    for load in loads:
        load.start()
    loads[0].wait()
    loads[1].wait()
    pl.semaphore_wait(barrier, len(peers))

    copies, drained = [], []

    def drain(last):
        for copy in copies[len(drained):-last]:
            copy.wait_send()
            drained.append(copy)

    def send(src, dst, peer):
        slot = len(copies)
        copy = pltpu.make_async_remote_copy(
            src_ref=src, dst_ref=dst, send_sem=send_sem.at[slot], recv_sem=recv_sem.at[slot],
            device_id=peer, device_id_type=pl.DeviceIdType.MESH,
        )
        copy.start()
        copies.append(copy)
        return copy

    def send_near(ref):
        return {d: send(ref, ref, y_peer[d]) for d in (2, 1, 3)}

    def send_plane(ref):
        return {at: send(ref, ref, xz_peer[at]) for at in steps}

    def wait_all(waits):
        for wait in waits:
            wait.wait_recv()

    def wait_near(near, part):
        passed = []
        for d in (1, 3, 2):
            near[d].wait_recv()
            there = part(step(y, Y - d, Y))
            passed.append(send(there, there, core_peer))
        return passed

    mine_w, mine_g = wp.at[0, x, zq, zr], gp.at[0, c, zh, y]
    far_g = send(mine_g, mine_g, zh_peer)
    far_w = send(mine_w, mine_w, zq_peer)
    near = send_near(mine_g)
    cross = [send(mine_g, mine_g, core_peer)]
    plane = send_plane(mine_w)
    for load in loads[2:]:
        load.wait()
    for i in range(X):
        turned = raw[i].reshape(xbins, C * cframes).T
        for j in range(C * ZH * Y):
            spec_t[i, j % C, pl.ds(j // C * grows, grows)] = turned[j * grows:(j + 1) * grows]
    cross += wait_near(near, lambda y_: gp.at[0, c, zh, y_])
    far_w.wait_recv()
    there = wp.at[0, x, 1 - zq, zr]
    plane_far = send_plane(there)
    far_g.wait_recv()
    wait_all(cross)
    there = gp.at[0, c, 1 - zh, y]
    far_near = send_near(there)
    cross = [send(there, there, core_peer)]
    wait_all(plane.values())
    cross += wait_near(far_near, lambda y_: gp.at[0, c, 1 - zh, y_])
    wait_all(plane_far.values())

    def acts_terms(it, c_, zh_, xs):
        w = halves(jnp.concatenate([wp[it, i].reshape(xbins, K) for i in xs], axis=0))
        if zh_ is None:
            g, rows = gp[it, c_].reshape(cframes, K), pl.ds(0, cframes)
        else:
            g, rows = gp[it, c_, zh_].reshape(Y * grows, K), pl.ds(zh_ * Y * grows, Y * grows)
        s = jnp.concatenate([spec_t[i, c_, rows] for i in xs], axis=1)
        return inner(halves(s / outer(halves(g), w)), w)

    def basis_terms(it, xs, c_):
        w = halves(jnp.concatenate([wp[it, i].reshape(xbins, K) for i in xs], axis=0))
        g = halves(gp[it + 1, c_].reshape(cframes, K))
        s = jnp.concatenate([spec[c_, i] for i in xs], axis=0)
        return inner(halves(s / outer(w, g)), g)

    half, tail = Y * grows, pl.ds(grows, 8)

    for it in range(ITERS):
        order = (0, 1) if it else (zh, 1 - zh)
        arrival = (0, 1) if it else (1 - zh, zh)
        others = [step(x, d, X) for d in (1, 3, 2)]

        def add_terms(c_, k, xs):
            terms = acts_terms(it, c_, order[k], xs)
            rows = pl.ds(0, half)
            fcore[it, c_, order[k], rows] = fcore[it, c_, order[k], rows] + terms if it else terms

        def send_core(k):
            rows = pl.ds(0, half if k else half + 8)
            return send(fcore.at[it, 1 - c, order[k], rows], fcore_in.at[it, order[k], rows], core_peer)

        def send_y(k, core):
            h, n = order[k], grows if k else grows + 8
            core.wait_recv()
            for i in range(Y):
                rows = pl.ds(i * grows, grows)
                fy[it, h, i, pl.ds(0, grows)] = fcore[it, c, h, rows] + fcore_in[it, h, rows]
                if k == 0:
                    rows = pl.ds(half, 8)
                    fy[it, h, i, tail] = fcore[it, c, h, rows] + fcore_in[it, h, rows]
            rows = pl.ds(0, n)
            return {
                d: send(fy.at[it, h, step(y, d, Y), rows], fy_in.at[it, h, d - 1, rows], y_peer[d])
                for d in (2, 1, 3)
            }

        def send_far(k, near):
            h, rows = order[k], pl.ds(0, grows if k else grows + 8)
            total = fy[it, h, y, rows]
            for d in (1, 3, 2):
                near[d].wait_recv()
                total = total + fy_in[it, h, d - 1, rows]
            fz[it, h, rows] = total
            return send(fz.at[it, h, rows], fz_in.at[it, h, rows], zh_peer)

        if it:
            wait_all(part[0, e] for part in plane_parts for e in range(1, ZR))
            for c_ in (1 - c, c):
                terms = acts_terms(it, c_, None, [x])
                for i in range(ZH):
                    fcore[it, c_, i, pl.ds(0, half)] = terms[i * half:(i + 1) * half]
            wait_all(part[at] for part in plane_parts for at in steps if at[0])
        sums = fold8(wp[it])
        for c_ in range(C):
            fcore[it, c_, order[0], pl.ds(half, 8)] = sums
        xs = others if it else [x, *others]
        add_terms(1 - c, 0, xs)
        core = [send_core(0)]
        if it:
            add_terms(1 - c, 1, xs)
            core.append(send_core(1))
            add_terms(c, 0, xs)
            near = [send_y(0, core[0])]
            add_terms(c, 1, xs)
        else:
            add_terms(c, 0, xs)
            wait_all(cross)
            add_terms(1 - c, 1, xs)
            core.append(send_core(1))
            near = [send_y(0, core[0])]
            add_terms(c, 1, xs)
        near.append(send_y(1, core[1]))
        far = [send_far(k, near[k]) for k in range(ZH)]
        drain(ZH)
        if it == 0:
            for i in range(X):
                for j in range(C):
                    spec[j, i] = spec_t[i, j].T
        near, cross = [], []
        for k in range(ZH):
            far[k].wait_recv()
            h = arrival[k]
            if k == 0:
                scale = jnp.sum(fz[it, order[0], tail] + fz_in[it, h, tail], axis=0)
            rows = pl.ds(0, grows)
            gp[it + 1, c, h, y] = gp[it, c, h, y] * (fz[it, h, rows] + fz_in[it, h, rows]) / scale
            mine = gp.at[it + 1, c, h, y]
            near.append(send_near(mine))
            cross.append(send(mine, mine, core_peer))
        if it + 1 == ITERS:
            acts_out[...] = gp[it + 1, c, zh, y]
        for k in range(ZH):
            cross += wait_near(near[k], lambda y_: gp.at[it + 1, c, arrival[k], y_])

        for i in range(0, X, GROUP):
            terms = basis_terms(it, range(i, i + GROUP), c)
            for j in range(GROUP):
                wacc[i + j] = terms[j * xbins:(j + 1) * xbins]
        sums = fold8(gp[it + 1, c])
        wait_all(cross)
        sums = sums + fold8(gp[it + 1, 1 - c])
        rt[it] = sums
        totals = {at: send(rt.at[it], rs_in.at[it, at[0], at[1]], xz_peer[at]) for at in steps}
        plane = {}
        sides = (1 - zq, zq) if it + 1 == ITERS else range(ZQ)
        for ds in PAIRS:
            xs = [step(x, d, X) for d in ds]
            both = basis_terms(it, xs, 1 - c)
            for n, x_ in enumerate(xs):
                terms = wacc[x_] + both[n * xbins:(n + 1) * xbins]
                rx[it, x_] = terms.reshape(ZQ, ZR, wrows, K)
            for k, j in enumerate(sides):
                for d, x_ in zip(ds, xs):
                    if it + 1 < ITERS:
                        for at in steps:
                            if at[0] == d:
                                src = rx.at[it, x_, j, step(zr, at[1], ZR)]
                                plane[k, at] = send(src, rx_in.at[at[0], j, at[1]], xz_peer[at])
                    elif d:
                        plane[k, d] = send(rx.at[it, x_, j], ex_in.at[d - 1, j], xz_peer[d, 0])
        for at in steps:
            totals[at].wait_recv()
            sums = sums + rs_in[it, at[0], at[1]]
        rs[it] = sums
        swap = send(rs.at[it], rs_in.at[it, 0, 0], zq_peer)
        if it + 1 < ITERS:
            far = []
            for j in range(ZQ):
                total = rx[it, x, j, zr]
                for at in sorted(steps):
                    plane[j, at].wait_recv()
                    total = total + rx_in[at[0], j, at[1]]
                rq[j] = total
                far.append(send(rq.at[j], rq_in.at[j], zq_peer))
            drain(1 + ZQ)
            swap.wait_recv()
            scale = jnp.sum(sums + rs_in[it, 0, 0], axis=0)
            plane_parts = []
            for j in range(ZQ):
                far[j].wait_recv()
                wp[it + 1, x, j, zr] = wp[it, x, j, zr] * (rq[j] + rq_in[j]) / scale
                plane_parts.append(send_plane(wp.at[it + 1, x, j, zr]))
        else:
            parts = {}
            for k, j in enumerate(sides):
                total = rx[it, x, j]
                for d in (1, 3, 2):
                    plane[k, d].wait_recv()
                    total = total + ex_in[d - 1, j]
                ez[j] = total
                for e in (2, 1, 3, 0):
                    if e or k == 0:
                        there = step(zr, e, ZR)
                        parts[k, e] = send(ez.at[j, there], ez_in.at[k, e], frame_at(j, there, x))
            drain(ZQ * ZR)
            swap.wait_recv()
            scale = jnp.sum(sums + rs_in[it, 0, 0], axis=0)
            total = ez[zq, zr]
            for k in (1, 0):
                for e in (1, 3, 2, 0):
                    if e or k == 0:
                        parts[k, e].wait_recv()
                        total = total + ez_in[k, e]
            basis_out[...] = wp[it, x, zq, zr] * total / scale

    for copy in copies[len(drained):]:
        copy.wait_send()


def write_out(basis_ref, acts_ref, basis_out, acts_out, sems):
    copies = [
        pltpu.make_async_copy(basis_ref, basis_out, sems.at[0]),
        pltpu.make_async_copy(acts_ref, acts_out, sems.at[1]),
    ]
    for copy in copies:
        copy.start()
    for copy in copies:
        copy.wait()


def per_device(spectrum, basis, activations):
    bins, frames = spectrum.shape
    wrows, grows = basis.shape[0], activations.shape[0]
    anywhere = pl.BlockSpec(memory_space=pl.ANY)
    vmem = pl.BlockSpec(memory_space=pltpu.VMEM)
    fresh = pl.pallas_call(
        kernel,
        out_shape=(
            pltpu.VMEM(basis.shape, F32),
            pltpu.VMEM(activations.shape, F32),
        ),
        in_specs=[anywhere] * 3,
        out_specs=(vmem, vmem),
        scratch_shapes=[
            pltpu.VMEM((X, ZQ * ZR, wrows, frames), F32),
            pltpu.VMEM((C, X, bins // X, frames // C), F32),
            pltpu.VMEM((X, C, frames // C, bins // X), F32),
            pltpu.VMEM((ITERS + 1, X, ZQ, ZR, wrows, K), F32),
            pltpu.VMEM((ITERS + 1, C, ZH, Y, grows, K), F32),
            pltpu.VMEM((ITERS, C, ZH, Y * grows + 8, K), F32),
            pltpu.VMEM((ITERS, ZH, Y * grows + 8, K), F32),
            pltpu.VMEM((ITERS, ZH, Y, grows + 8, K), F32),
            pltpu.VMEM((ITERS, ZH, Y - 1, grows + 8, K), F32),
            pltpu.VMEM((ITERS, ZH, grows + 8, K), F32),
            pltpu.VMEM((ITERS, ZH, grows + 8, K), F32),
            pltpu.VMEM((X, bins // X, K), F32),
            pltpu.VMEM((ITERS, X, ZQ, ZR, wrows, K), F32),
            pltpu.VMEM((X, ZQ, ZR, wrows, K), F32),
            pltpu.VMEM((ITERS, 8, K), F32),
            pltpu.VMEM((ITERS, 8, K), F32),
            pltpu.VMEM((ITERS, X, ZR, 8, K), F32),
            pltpu.VMEM((ZQ, wrows, K), F32),
            pltpu.VMEM((ZQ, wrows, K), F32),
            pltpu.VMEM((X - 1, ZQ, ZR, wrows, K), F32),
            pltpu.VMEM((ZQ, ZR, wrows, K), F32),
            pltpu.VMEM((ZQ, ZR, wrows, K), F32),
            pltpu.SemaphoreType.DMA((2 + X,)),
            pltpu.SemaphoreType.DMA((SEMS,)),
            pltpu.SemaphoreType.DMA((SEMS,)),
        ],
        compiler_params=pltpu.CompilerParams(
            collective_id=0, has_side_effects=True, vmem_limit_bytes=62914560
        ),
    )(spectrum.reshape(ZQ * ZR, X, wrows, frames), basis, activations)
    return pl.pallas_call(
        write_out,
        out_shape=(
            jax.ShapeDtypeStruct(basis.shape, F32),
            jax.ShapeDtypeStruct(activations.shape, F32),
        ),
        in_specs=[vmem, vmem],
        out_specs=(anywhere, anywhere),
        scratch_shapes=[pltpu.SemaphoreType.DMA((2,))],
        compiler_params=pltpu.CompilerParams(vmem_limit_bytes=1 << 20),
    )(*fresh)


def solution(mesh):
    return jax.shard_map(
        per_device,
        mesh=mesh,
        in_specs=(P("freq", "frame"), P(("freq", "frame"), None), P(("frame", "freq"), None)),
        out_specs=(P(("freq", "frame"), None), P(("frame", "freq"), None)),
        check_vma=False,
    )
```

```python
import jax
import jax.numpy as jnp
from jax import lax
from jax.experimental import pallas as pl
from jax.experimental.pallas import tpu as pltpu
from jax.sharding import PartitionSpec as P

ITERS = 2
K = 128
X, ZR, ZQ = 4, 4, 2
Y, ZH, C = 4, 2, 2
SEMS = 224
GROUP = 2
PAIRS = ((2, 1), (3, 0))
F32, BF16 = jnp.float32, jnp.bfloat16


def halves(value):
    high = value.astype(BF16)
    return high, (value - high.astype(F32)).astype(BF16)


def dot(left, right, contract_right):
    return lax.dot_general(
        left, right, (((1,), (contract_right,)), ((), ())), preferred_element_type=F32
    )


def outer(left, right):
    wide = dot(jnp.concatenate(left, axis=1), jnp.concatenate([right[0], right[0]], axis=1), 1)
    return wide + dot(left[0], right[1], 1)


def inner(left, right):
    wide = dot(left[0], jnp.concatenate(right, axis=1), 0)
    return wide[:, :K] + wide[:, K:] + dot(left[1], right[0], 0)


def fold8(value):
    return jnp.sum(value.reshape(-1, 8, K), axis=0)


def kernel(
    spec_hbm, basis_hbm, acts_hbm, basis_out, acts_out,
    raw, spec, spec_t, wp, gp,
    fcore, fcore_in, fy, fy_in, fz, fz_in,
    wacc, rx, rx_in, rt, rs, rs_in, rq, rq_in, ex_in, ez, ez_in,
    load_sem, send_sem, recv_sem,
):
    fr = lax.axis_index("frame")
    fq = lax.axis_index("freq")
    x, zl = lax.rem(fr, X), lax.div(fr, X)
    zr, zq = lax.rem(zl, ZR), lax.div(zl, ZR)
    c, yz = lax.rem(fq, C), lax.div(fq, C)
    y, zh = lax.rem(yz, Y), lax.div(yz, Y)
    wrows, grows = basis_hbm.shape[0], acts_hbm.shape[0]
    xbins, cframes = ZQ * ZR * wrows, ZH * Y * grows

    def frame_at(zq_, zr_, x_):
        return ((zq_ * ZR + zr_) * X + x_, fq)

    def freq_at(zh_, y_, c_):
        return (fr, (zh_ * Y + y_) * C + c_)

    def step(value, by, size):
        return lax.rem(value + by, size)

    core_peer = freq_at(zh, y, 1 - c)
    zh_peer = freq_at(1 - zh, y, c)
    zh_other = freq_at(1 - zh, y, 1 - c)
    zq_peer = frame_at(1 - zq, zr, x)
    y_peer = {d: freq_at(zh, step(y, d, Y), c) for d in (2, 1, 3)}
    steps = [(d, e) for d in (2, 1, 3, 0) for e in (2, 1, 3, 0) if d or e]
    xz_peer = {(d, e): frame_at(zq, step(zr, e, ZR), step(x, d, X)) for d, e in steps}
    peers = [zh_peer, zh_other, zq_peer, *xz_peer.values(), *y_peer.values(), core_peer]

    barrier = pltpu.get_barrier_semaphore()
    for peer in peers:
        pl.semaphore_signal(barrier, inc=1, device_id=peer, device_id_type=pl.DeviceIdType.MESH)

    loads = [
        pltpu.make_async_copy(acts_hbm, gp.at[0, c, zh, y], load_sem.at[0]),
        pltpu.make_async_copy(basis_hbm, wp.at[0, x, zq, zr], load_sem.at[1]),
    ]
    for i in range(X):
        loads.append(pltpu.make_async_copy(spec_hbm.at[:, i], raw.at[i], load_sem.at[2 + i]))
    for load in loads:
        load.start()
    loads[0].wait()
    loads[1].wait()
    pl.semaphore_wait(barrier, len(peers))

    copies, drained = [], []

    def drain(last):
        for copy in copies[len(drained):-last]:
            copy.wait_send()
            drained.append(copy)

    def send(src, dst, peer):
        slot = len(copies)
        copy = pltpu.make_async_remote_copy(
            src_ref=src, dst_ref=dst, send_sem=send_sem.at[slot], recv_sem=recv_sem.at[slot],
            device_id=peer, device_id_type=pl.DeviceIdType.MESH,
        )
        copy.start()
        copies.append(copy)
        return copy

    def send_near(ref):
        return {d: send(ref, ref, y_peer[d]) for d in (2, 1, 3)}

    def send_plane(ref):
        return {at: send(ref, ref, xz_peer[at]) for at in steps}

    def wait_all(waits):
        for wait in waits:
            wait.wait_recv()

    def wait_near(near, part):
        passed = []
        for d in (1, 3, 2):
            near[d].wait_recv()
            there = part(step(y, Y - d, Y))
            passed.append(send(there, there, core_peer))
        return passed

    mine_w, mine_g = wp.at[0, x, zq, zr], gp.at[0, c, zh, y]
    far_g = [send(mine_g, mine_g, zh_peer), send(mine_g, mine_g, zh_other)]
    far_w = send(mine_w, mine_w, zq_peer)
    near = send_near(mine_g)
    cross = [send(mine_g, mine_g, core_peer)]
    plane = send_plane(mine_w)
    for load in loads[2:]:
        load.wait()
    for i in range(X):
        turned = raw[i].reshape(xbins, C * cframes).T
        for j in range(C * ZH * Y):
            spec_t[i, j % C, pl.ds(j // C * grows, grows)] = turned[j * grows:(j + 1) * grows]
    cross += wait_near(near, lambda y_: gp.at[0, c, zh, y_])
    far_w.wait_recv()
    there = wp.at[0, x, 1 - zq, zr]
    plane_far = send_plane(there)
    wait_all(far_g)
    far_near = send_near(gp.at[0, :, 1 - zh, y])
    wait_all(plane.values())
    wait_all(cross)
    wait_all(plane_far.values())

    def acts_terms(it, c_, zh_, xs):
        w = halves(jnp.concatenate([wp[it, i].reshape(xbins, K) for i in xs], axis=0))
        if zh_ is None:
            g, rows = gp[it, c_].reshape(cframes, K), pl.ds(0, cframes)
        else:
            g, rows = gp[it, c_, zh_].reshape(Y * grows, K), pl.ds(zh_ * Y * grows, Y * grows)
        s = jnp.concatenate([spec_t[i, c_, rows] for i in xs], axis=1)
        return inner(halves(s / outer(halves(g), w)), w)

    def basis_terms(it, xs, c_):
        w = halves(jnp.concatenate([wp[it, i].reshape(xbins, K) for i in xs], axis=0))
        g = halves(gp[it + 1, c_].reshape(cframes, K))
        s = jnp.concatenate([spec[c_, i] for i in xs], axis=0)
        return inner(halves(s / outer(w, g)), g)

    half, tail = Y * grows, pl.ds(grows, 8)

    for it in range(ITERS):
        order = (0, 1) if it else (zh, 1 - zh)
        arrival = (0, 1) if it else (1 - zh, zh)
        others = [step(x, d, X) for d in (1, 3, 2)]

        def add_terms(c_, k, xs):
            terms = acts_terms(it, c_, order[k], xs)
            rows = pl.ds(0, half)
            fcore[it, c_, order[k], rows] = fcore[it, c_, order[k], rows] + terms if it else terms

        def send_core(k):
            rows = pl.ds(0, half if k else half + 8)
            return send(fcore.at[it, 1 - c, order[k], rows], fcore_in.at[it, order[k], rows], core_peer)

        def send_y(k, core):
            h, n = order[k], grows if k else grows + 8
            core.wait_recv()
            for i in range(Y):
                rows = pl.ds(i * grows, grows)
                fy[it, h, i, pl.ds(0, grows)] = fcore[it, c, h, rows] + fcore_in[it, h, rows]
                if k == 0:
                    rows = pl.ds(half, 8)
                    fy[it, h, i, tail] = fcore[it, c, h, rows] + fcore_in[it, h, rows]
            rows = pl.ds(0, n)
            return {
                d: send(fy.at[it, h, step(y, d, Y), rows], fy_in.at[it, h, d - 1, rows], y_peer[d])
                for d in (2, 1, 3)
            }

        def send_far(k, near):
            h, rows = order[k], pl.ds(0, grows if k else grows + 8)
            total = fy[it, h, y, rows]
            for d in (1, 3, 2):
                near[d].wait_recv()
                total = total + fy_in[it, h, d - 1, rows]
            fz[it, h, rows] = total
            return send(fz.at[it, h, rows], fz_in.at[it, h, rows], zh_peer)

        if it:
            wait_all(part[0, e] for part in plane_parts for e in range(1, ZR))
            for c_ in (1 - c, c):
                terms = acts_terms(it, c_, None, [x])
                for i in range(ZH):
                    fcore[it, c_, i, pl.ds(0, half)] = terms[i * half:(i + 1) * half]
            wait_all(part[at] for part in plane_parts for at in steps if at[0])
        sums = fold8(wp[it])
        for c_ in range(C):
            fcore[it, c_, order[0], pl.ds(half, 8)] = sums
        xs = others if it else [x, *others]
        add_terms(1 - c, 0, xs)
        core = [send_core(0)]
        if it:
            add_terms(1 - c, 1, xs)
            core.append(send_core(1))
            add_terms(c, 0, xs)
            near = [send_y(0, core[0])]
            add_terms(c, 1, xs)
        else:
            add_terms(c, 0, xs)
            wait_all(far_near.values())
            add_terms(1 - c, 1, xs)
            core.append(send_core(1))
            near = [send_y(0, core[0])]
            add_terms(c, 1, xs)
        near.append(send_y(1, core[1]))
        far = [send_far(k, near[k]) for k in range(ZH)]
        drain(ZH)
        if it == 0:
            for i in range(X):
                for j in range(C):
                    spec[j, i] = spec_t[i, j].T
        near, cross = [], []
        for k in range(ZH):
            far[k].wait_recv()
            h = arrival[k]
            if k == 0:
                scale = jnp.sum(fz[it, order[0], tail] + fz_in[it, h, tail], axis=0)
            rows = pl.ds(0, grows)
            gp[it + 1, c, h, y] = gp[it, c, h, y] * (fz[it, h, rows] + fz_in[it, h, rows]) / scale
            mine = gp.at[it + 1, c, h, y]
            near.append(send_near(mine))
            cross.append(send(mine, mine, core_peer))
        if it + 1 == ITERS:
            acts_out[...] = gp[it + 1, c, zh, y]
        for k in range(ZH):
            cross += wait_near(near[k], lambda y_: gp.at[it + 1, c, arrival[k], y_])

        for i in range(0, X, GROUP):
            terms = basis_terms(it, range(i, i + GROUP), c)
            for j in range(GROUP):
                wacc[i + j] = terms[j * xbins:(j + 1) * xbins]
        sums = fold8(gp[it + 1, c])
        wait_all(cross)
        plane = {}
        sides = (1 - zq, zq) if it + 1 == ITERS else range(ZQ)
        for ds in PAIRS:
            xs = [step(x, d, X) for d in ds]
            both = basis_terms(it, xs, 1 - c)
            for n, x_ in enumerate(xs):
                terms = wacc[x_] + both[n * xbins:(n + 1) * xbins]
                rx[it, x_] = terms.reshape(ZQ, ZR, wrows, K)
            for k, j in enumerate(sides):
                for d, x_ in zip(ds, xs):
                    if it + 1 < ITERS:
                        for at in steps:
                            if at[0] == d:
                                src = rx.at[it, x_, j, step(zr, at[1], ZR)]
                                plane[k, at] = send(src, rx_in.at[at[0], j, at[1]], xz_peer[at])
                    elif d:
                        plane[k, d] = send(rx.at[it, x_, j], ex_in.at[d - 1, j], xz_peer[d, 0])
            if ds is PAIRS[0]:
                sums = sums + fold8(gp[it + 1, 1 - c])
                rt[it] = sums
                totals = {at: send(rt.at[it], rs_in.at[it, at[0], at[1]], xz_peer[at]) for at in steps}
        for at in steps:
            totals[at].wait_recv()
            sums = sums + rs_in[it, at[0], at[1]]
        rs[it] = sums
        swap = send(rs.at[it], rs_in.at[it, 0, 0], zq_peer)
        if it + 1 < ITERS:
            far = []
            for j in range(ZQ):
                total = rx[it, x, j, zr]
                for at in sorted(steps):
                    plane[j, at].wait_recv()
                    total = total + rx_in[at[0], j, at[1]]
                rq[j] = total
                far.append(send(rq.at[j], rq_in.at[j], zq_peer))
            drain(1 + ZQ)
            swap.wait_recv()
            scale = jnp.sum(sums + rs_in[it, 0, 0], axis=0)
            plane_parts = []
            for j in range(ZQ):
                far[j].wait_recv()
                wp[it + 1, x, j, zr] = wp[it, x, j, zr] * (rq[j] + rq_in[j]) / scale
                plane_parts.append(send_plane(wp.at[it + 1, x, j, zr]))
        else:
            parts = {}
            for k, j in enumerate(sides):
                total = rx[it, x, j]
                for d in (1, 3, 2):
                    plane[k, d].wait_recv()
                    total = total + ex_in[d - 1, j]
                ez[j] = total
                for e in (2, 1, 3, 0):
                    if e or k == 0:
                        there = step(zr, e, ZR)
                        parts[k, e] = send(ez.at[j, there], ez_in.at[k, e], frame_at(j, there, x))
            drain(ZQ * ZR)
            swap.wait_recv()
            scale = jnp.sum(sums + rs_in[it, 0, 0], axis=0)
            total = ez[zq, zr]
            for k in (1, 0):
                for e in (1, 3, 2, 0):
                    if e or k == 0:
                        parts[k, e].wait_recv()
                        total = total + ez_in[k, e]
            basis_out[...] = wp[it, x, zq, zr] * total / scale

    for copy in copies[len(drained):]:
        copy.wait_send()


def write_out(basis_ref, acts_ref, basis_out, acts_out, sems):
    copies = [
        pltpu.make_async_copy(basis_ref, basis_out, sems.at[0]),
        pltpu.make_async_copy(acts_ref, acts_out, sems.at[1]),
    ]
    for copy in copies:
        copy.start()
    for copy in copies:
        copy.wait()


def per_device(spectrum, basis, activations):
    bins, frames = spectrum.shape
    wrows, grows = basis.shape[0], activations.shape[0]
    anywhere = pl.BlockSpec(memory_space=pl.ANY)
    vmem = pl.BlockSpec(memory_space=pltpu.VMEM)
    fresh = pl.pallas_call(
        kernel,
        out_shape=(
            pltpu.VMEM(basis.shape, F32),
            pltpu.VMEM(activations.shape, F32),
        ),
        in_specs=[anywhere] * 3,
        out_specs=(vmem, vmem),
        scratch_shapes=[
            pltpu.VMEM((X, ZQ * ZR, wrows, frames), F32),
            pltpu.VMEM((C, X, bins // X, frames // C), F32),
            pltpu.VMEM((X, C, frames // C, bins // X), F32),
            pltpu.VMEM((ITERS + 1, X, ZQ, ZR, wrows, K), F32),
            pltpu.VMEM((ITERS + 1, C, ZH, Y, grows, K), F32),
            pltpu.VMEM((ITERS, C, ZH, Y * grows + 8, K), F32),
            pltpu.VMEM((ITERS, ZH, Y * grows + 8, K), F32),
            pltpu.VMEM((ITERS, ZH, Y, grows + 8, K), F32),
            pltpu.VMEM((ITERS, ZH, Y - 1, grows + 8, K), F32),
            pltpu.VMEM((ITERS, ZH, grows + 8, K), F32),
            pltpu.VMEM((ITERS, ZH, grows + 8, K), F32),
            pltpu.VMEM((X, bins // X, K), F32),
            pltpu.VMEM((ITERS, X, ZQ, ZR, wrows, K), F32),
            pltpu.VMEM((X, ZQ, ZR, wrows, K), F32),
            pltpu.VMEM((ITERS, 8, K), F32),
            pltpu.VMEM((ITERS, 8, K), F32),
            pltpu.VMEM((ITERS, X, ZR, 8, K), F32),
            pltpu.VMEM((ZQ, wrows, K), F32),
            pltpu.VMEM((ZQ, wrows, K), F32),
            pltpu.VMEM((X - 1, ZQ, ZR, wrows, K), F32),
            pltpu.VMEM((ZQ, ZR, wrows, K), F32),
            pltpu.VMEM((ZQ, ZR, wrows, K), F32),
            pltpu.SemaphoreType.DMA((2 + X,)),
            pltpu.SemaphoreType.DMA((SEMS,)),
            pltpu.SemaphoreType.DMA((SEMS,)),
        ],
        compiler_params=pltpu.CompilerParams(
            collective_id=0, has_side_effects=True, vmem_limit_bytes=62914560
        ),
    )(spectrum.reshape(ZQ * ZR, X, wrows, frames), basis, activations)
    return pl.pallas_call(
        write_out,
        out_shape=(
            jax.ShapeDtypeStruct(basis.shape, F32),
            jax.ShapeDtypeStruct(activations.shape, F32),
        ),
        in_specs=[vmem, vmem],
        out_specs=(anywhere, anywhere),
        scratch_shapes=[pltpu.SemaphoreType.DMA((2,))],
        compiler_params=pltpu.CompilerParams(vmem_limit_bytes=1 << 20),
    )(*fresh)


def solution(mesh):
    return jax.shard_map(
        per_device,
        mesh=mesh,
        in_specs=(P("freq", "frame"), P(("freq", "frame"), None), P(("frame", "freq"), None)),
        out_specs=(P(("freq", "frame"), None), P(("frame", "freq"), None)),
        check_vma=False,
    )
```

```python
import jax
import jax.numpy as jnp
from jax import lax
from jax.experimental import pallas as pl
from jax.experimental.pallas import tpu as pltpu
from jax.sharding import PartitionSpec as P

ITERS = 2
K = 128
X, ZR, ZQ = 4, 4, 2
Y, ZH, C = 4, 2, 2
SEMS = 240
GROUP = 2
PAIRS = ((2, 1), (3, 0))
F32, BF16 = jnp.float32, jnp.bfloat16


def halves(value):
    high = value.astype(BF16)
    return high, (value - high.astype(F32)).astype(BF16)


def dot(left, right, contract_right):
    return lax.dot_general(
        left, right, (((1,), (contract_right,)), ((), ())), preferred_element_type=F32
    )


def outer(left, right):
    wide = dot(jnp.concatenate(left, axis=1), jnp.concatenate([right[0], right[0]], axis=1), 1)
    return wide + dot(left[0], right[1], 1)


def inner(left, right):
    wide = dot(left[0], jnp.concatenate(right, axis=1), 0)
    return wide[:, :K] + wide[:, K:] + dot(left[1], right[0], 0)


def fold8(value):
    return jnp.sum(value.reshape(-1, 8, K), axis=0)


def kernel(
    spec_hbm, basis_hbm, acts_hbm, basis_out, acts_out,
    raw, spec, spec_t, wp, gp,
    st, st_in, su, su_in, fcore, fcore_in, fy, fy_in, fz, fz_in,
    wacc, rx, rx_in, rt, rs, rs_in, rq, rq_in, ex_in, ez, ez_in,
    load_sem, send_sem, recv_sem,
):
    fr = lax.axis_index("frame")
    fq = lax.axis_index("freq")
    x, zl = lax.rem(fr, X), lax.div(fr, X)
    zr, zq = lax.rem(zl, ZR), lax.div(zl, ZR)
    c, yz = lax.rem(fq, C), lax.div(fq, C)
    y, zh = lax.rem(yz, Y), lax.div(yz, Y)
    wrows, grows = basis_hbm.shape[0], acts_hbm.shape[0]
    xbins, cframes = ZQ * ZR * wrows, ZH * Y * grows

    def frame_at(zq_, zr_, x_):
        return ((zq_ * ZR + zr_) * X + x_, fq)

    def freq_at(zh_, y_, c_):
        return (fr, (zh_ * Y + y_) * C + c_)

    def step(value, by, size):
        return lax.rem(value + by, size)

    core_peer = freq_at(zh, y, 1 - c)
    zh_peer = freq_at(1 - zh, y, c)
    zq_peer = frame_at(1 - zq, zr, x)
    y_peer = {d: freq_at(zh, step(y, d, Y), c) for d in (2, 1, 3)}
    steps = [(d, e) for d in (2, 1, 3, 0) for e in (2, 1, 3, 0) if d or e]
    xz_peer = {(d, e): frame_at(zq, step(zr, e, ZR), step(x, d, X)) for d, e in steps}
    cells = [(d, e) for d in (2, 1, 3, 0) for e in (0, 1) if d or e]
    cell_peer = {(d, e): freq_at(zh, step(y, d, Y), 1 - c if e else c) for d, e in cells}
    peers = [zh_peer, zq_peer, *xz_peer.values(), *y_peer.values(), core_peer]

    barrier = pltpu.get_barrier_semaphore()
    for peer in peers:
        pl.semaphore_signal(barrier, inc=1, device_id=peer, device_id_type=pl.DeviceIdType.MESH)

    loads = [
        pltpu.make_async_copy(acts_hbm, gp.at[0, c, zh, y], load_sem.at[0]),
        pltpu.make_async_copy(basis_hbm, wp.at[0, x, zq, zr], load_sem.at[1]),
    ]
    for i in range(X):
        loads.append(pltpu.make_async_copy(spec_hbm.at[:, i], raw.at[i], load_sem.at[2 + i]))
    for load in loads:
        load.start()
    loads[0].wait()
    loads[1].wait()
    pl.semaphore_wait(barrier, len(peers))

    copies, drained = [], []

    def drain(last):
        for copy in copies[len(drained):-last]:
            copy.wait_send()
            drained.append(copy)

    def send(src, dst, peer):
        slot = len(copies)
        copy = pltpu.make_async_remote_copy(
            src_ref=src, dst_ref=dst, send_sem=send_sem.at[slot], recv_sem=recv_sem.at[slot],
            device_id=peer, device_id_type=pl.DeviceIdType.MESH,
        )
        copy.start()
        copies.append(copy)
        return copy

    def send_near(ref):
        return {d: send(ref, ref, y_peer[d]) for d in (2, 1, 3)}

    def send_plane(ref):
        return {at: send(ref, ref, xz_peer[at]) for at in steps}

    def wait_all(waits):
        for wait in waits:
            wait.wait_recv()

    def wait_near(near, part):
        passed = []
        for d in (1, 3, 2):
            near[d].wait_recv()
            there = part(step(y, Y - d, Y))
            passed.append(send(there, there, core_peer))
        return passed

    mine_w, mine_g = wp.at[0, x, zq, zr], gp.at[0, c, zh, y]
    far_g = send(mine_g, mine_g, zh_peer)
    far_w = send(mine_w, mine_w, zq_peer)
    near = send_near(mine_g)
    cross = [send(mine_g, mine_g, core_peer)]
    plane = send_plane(mine_w)
    for load in loads[2:]:
        load.wait()
    for i in range(X):
        turned = raw[i].reshape(xbins, C * cframes).T
        for j in range(C * ZH * Y):
            spec_t[i, j % C, pl.ds(j // C * grows, grows)] = turned[j * grows:(j + 1) * grows]
    cross += wait_near(near, lambda y_: gp.at[0, c, zh, y_])
    far_w.wait_recv()
    there = wp.at[0, x, 1 - zq, zr]
    plane_far = send_plane(there)
    far_g.wait_recv()
    wait_all(cross)
    there = gp.at[0, c, 1 - zh, y]
    far_near = send_near(there)
    cross = [send(there, there, core_peer)]
    wait_all(plane.values())
    cross += wait_near(far_near, lambda y_: gp.at[0, c, 1 - zh, y_])
    wait_all(plane_far.values())

    def acts_terms(it, c_, zh_, xs):
        w = halves(jnp.concatenate([wp[it, i].reshape(xbins, K) for i in xs], axis=0))
        if zh_ is None:
            g, rows = gp[it, c_].reshape(cframes, K), pl.ds(0, cframes)
        else:
            g, rows = gp[it, c_, zh_].reshape(Y * grows, K), pl.ds(zh_ * Y * grows, Y * grows)
        s = jnp.concatenate([spec_t[i, c_, rows] for i in xs], axis=1)
        return inner(halves(s / outer(halves(g), w)), w)

    def basis_terms(it, xs, c_):
        w = halves(jnp.concatenate([wp[it, i].reshape(xbins, K) for i in xs], axis=0))
        g = halves(gp[it + 1, c_].reshape(cframes, K))
        s = jnp.concatenate([spec[c_, i] for i in xs], axis=0)
        return inner(halves(s / outer(w, g)), g)

    half = Y * grows

    for it in range(ITERS):
        order = (0, 1) if it else (zh, 1 - zh)
        arrival = (0, 1) if it else (1 - zh, zh)
        others = [step(x, d, X) for d in (1, 3, 2)]

        def add_terms(c_, k, xs):
            terms = acts_terms(it, c_, order[k], xs)
            rows = pl.ds(0, half)
            fcore[it, c_, order[k], rows] = fcore[it, c_, order[k], rows] + terms if it else terms

        def send_core(k):
            return send(fcore.at[it, 1 - c, order[k]], fcore_in.at[it, order[k]], core_peer)

        def send_totals():
            st[it] = fold8(wp[it])
            return st[it], {
                at: send(st.at[it], st_in.at[it, at[0], at[1]], cell_peer[at]) for at in cells
            }

        def send_y(k, core):
            h = order[k]
            core.wait_recv()
            for i in range(Y):
                rows = pl.ds(i * grows, grows)
                fy[it, h, i] = fcore[it, c, h, rows] + fcore_in[it, h, rows]
            return {
                d: send(fy.at[it, h, step(y, d, Y)], fy_in.at[it, h, d - 1], y_peer[d])
                for d in (2, 1, 3)
            }

        def send_far(k, near):
            h = order[k]
            total = fy[it, h, y]
            for d in (1, 3, 2):
                near[d].wait_recv()
                total = total + fy_in[it, h, d - 1]
            fz[it, h] = total
            return send(fz.at[it, h], fz_in.at[it, h], zh_peer)

        if it:
            wait_all(part[0, e] for part in plane_parts for e in range(1, ZR))
            for c_ in (1 - c, c):
                terms = acts_terms(it, c_, None, [x])
                for i in range(ZH):
                    fcore[it, c_, i, pl.ds(0, half)] = terms[i * half:(i + 1) * half]
            wait_all(part[at] for part in plane_parts for at in steps if at[0])
        xs = others if it else [x, *others]
        add_terms(1 - c, 0, xs)
        core = [send_core(0)]
        if it:
            add_terms(1 - c, 1, xs)
            core.append(send_core(1))
            sums, totals = send_totals()
            add_terms(c, 0, xs)
            near = [send_y(0, core[0])]
            add_terms(c, 1, xs)
        else:
            sums, totals = send_totals()
            add_terms(c, 0, xs)
            wait_all(cross)
            add_terms(1 - c, 1, xs)
            core.append(send_core(1))
            near = [send_y(0, core[0])]
            add_terms(c, 1, xs)
        near.append(send_y(1, core[1]))
        for at in cells:
            totals[at].wait_recv()
            sums = sums + st_in[it, at[0], at[1]]
        su[it] = sums
        swap = send(su.at[it], su_in.at[it], zh_peer)
        far = [send_far(k, near[k]) for k in range(ZH)]
        drain(ZH)
        if it == 0:
            for i in range(X):
                for j in range(C):
                    spec[j, i] = spec_t[i, j].T
        near, cross = [], []
        for k in range(ZH):
            far[k].wait_recv()
            h = arrival[k]
            if k == 0:
                swap.wait_recv()
                scale = jnp.sum(su[it] + su_in[it], axis=0)
            gp[it + 1, c, h, y] = gp[it, c, h, y] * (fz[it, h] + fz_in[it, h]) / scale
            mine = gp.at[it + 1, c, h, y]
            near.append(send_near(mine))
            cross.append(send(mine, mine, core_peer))
        if it + 1 == ITERS:
            acts_out[...] = gp[it + 1, c, zh, y]
        for k in range(ZH):
            cross += wait_near(near[k], lambda y_: gp.at[it + 1, c, arrival[k], y_])

        for i in range(0, X, GROUP):
            terms = basis_terms(it, range(i, i + GROUP), c)
            for j in range(GROUP):
                wacc[i + j] = terms[j * xbins:(j + 1) * xbins]
        sums = fold8(gp[it + 1, c])
        wait_all(cross)
        sums = sums + fold8(gp[it + 1, 1 - c])
        rt[it] = sums
        totals = {at: send(rt.at[it], rs_in.at[it, at[0], at[1]], xz_peer[at]) for at in steps}
        plane = {}
        sides = (1 - zq, zq) if it + 1 == ITERS else range(ZQ)
        for ds in PAIRS:
            xs = [step(x, d, X) for d in ds]
            both = basis_terms(it, xs, 1 - c)
            for n, x_ in enumerate(xs):
                terms = wacc[x_] + both[n * xbins:(n + 1) * xbins]
                rx[it, x_] = terms.reshape(ZQ, ZR, wrows, K)
            for k, j in enumerate(sides):
                for d, x_ in zip(ds, xs):
                    if it + 1 < ITERS:
                        for at in steps:
                            if at[0] == d:
                                src = rx.at[it, x_, j, step(zr, at[1], ZR)]
                                plane[k, at] = send(src, rx_in.at[at[0], j, at[1]], xz_peer[at])
                    elif d:
                        plane[k, d] = send(rx.at[it, x_, j], ex_in.at[d - 1, j], xz_peer[d, 0])
        for at in steps:
            totals[at].wait_recv()
            sums = sums + rs_in[it, at[0], at[1]]
        rs[it] = sums
        swap = send(rs.at[it], rs_in.at[it, 0, 0], zq_peer)
        if it + 1 < ITERS:
            far = []
            for j in range(ZQ):
                total = rx[it, x, j, zr]
                for at in sorted(steps):
                    plane[j, at].wait_recv()
                    total = total + rx_in[at[0], j, at[1]]
                rq[j] = total
                far.append(send(rq.at[j], rq_in.at[j], zq_peer))
            drain(1 + ZQ)
            swap.wait_recv()
            scale = jnp.sum(sums + rs_in[it, 0, 0], axis=0)
            plane_parts = []
            for j in range(ZQ):
                far[j].wait_recv()
                wp[it + 1, x, j, zr] = wp[it, x, j, zr] * (rq[j] + rq_in[j]) / scale
                plane_parts.append(send_plane(wp.at[it + 1, x, j, zr]))
        else:
            parts = {}
            for k, j in enumerate(sides):
                total = rx[it, x, j]
                for d in (1, 3, 2):
                    plane[k, d].wait_recv()
                    total = total + ex_in[d - 1, j]
                ez[j] = total
                for e in (2, 1, 3, 0):
                    if e or k == 0:
                        there = step(zr, e, ZR)
                        parts[k, e] = send(ez.at[j, there], ez_in.at[k, e], frame_at(j, there, x))
            drain(ZQ * ZR)
            swap.wait_recv()
            scale = jnp.sum(sums + rs_in[it, 0, 0], axis=0)
            total = ez[zq, zr]
            for k in (1, 0):
                for e in (1, 3, 2, 0):
                    if e or k == 0:
                        parts[k, e].wait_recv()
                        total = total + ez_in[k, e]
            basis_out[...] = wp[it, x, zq, zr] * total / scale

    for copy in copies[len(drained):]:
        copy.wait_send()


def write_out(basis_ref, acts_ref, basis_out, acts_out, sems):
    copies = [
        pltpu.make_async_copy(basis_ref, basis_out, sems.at[0]),
        pltpu.make_async_copy(acts_ref, acts_out, sems.at[1]),
    ]
    for copy in copies:
        copy.start()
    for copy in copies:
        copy.wait()


def per_device(spectrum, basis, activations):
    bins, frames = spectrum.shape
    wrows, grows = basis.shape[0], activations.shape[0]
    anywhere = pl.BlockSpec(memory_space=pl.ANY)
    vmem = pl.BlockSpec(memory_space=pltpu.VMEM)
    fresh = pl.pallas_call(
        kernel,
        out_shape=(
            pltpu.VMEM(basis.shape, F32),
            pltpu.VMEM(activations.shape, F32),
        ),
        in_specs=[anywhere] * 3,
        out_specs=(vmem, vmem),
        scratch_shapes=[
            pltpu.VMEM((X, ZQ * ZR, wrows, frames), F32),
            pltpu.VMEM((C, X, bins // X, frames // C), F32),
            pltpu.VMEM((X, C, frames // C, bins // X), F32),
            pltpu.VMEM((ITERS + 1, X, ZQ, ZR, wrows, K), F32),
            pltpu.VMEM((ITERS + 1, C, ZH, Y, grows, K), F32),
            pltpu.VMEM((ITERS, 8, K), F32),
            pltpu.VMEM((ITERS, Y, C, 8, K), F32),
            pltpu.VMEM((ITERS, 8, K), F32),
            pltpu.VMEM((ITERS, 8, K), F32),
            pltpu.VMEM((ITERS, C, ZH, Y * grows, K), F32),
            pltpu.VMEM((ITERS, ZH, Y * grows, K), F32),
            pltpu.VMEM((ITERS, ZH, Y, grows, K), F32),
            pltpu.VMEM((ITERS, ZH, Y - 1, grows, K), F32),
            pltpu.VMEM((ITERS, ZH, grows, K), F32),
            pltpu.VMEM((ITERS, ZH, grows, K), F32),
            pltpu.VMEM((X, bins // X, K), F32),
            pltpu.VMEM((ITERS, X, ZQ, ZR, wrows, K), F32),
            pltpu.VMEM((X, ZQ, ZR, wrows, K), F32),
            pltpu.VMEM((ITERS, 8, K), F32),
            pltpu.VMEM((ITERS, 8, K), F32),
            pltpu.VMEM((ITERS, X, ZR, 8, K), F32),
            pltpu.VMEM((ZQ, wrows, K), F32),
            pltpu.VMEM((ZQ, wrows, K), F32),
            pltpu.VMEM((X - 1, ZQ, ZR, wrows, K), F32),
            pltpu.VMEM((ZQ, ZR, wrows, K), F32),
            pltpu.VMEM((ZQ, ZR, wrows, K), F32),
            pltpu.SemaphoreType.DMA((2 + X,)),
            pltpu.SemaphoreType.DMA((SEMS,)),
            pltpu.SemaphoreType.DMA((SEMS,)),
        ],
        compiler_params=pltpu.CompilerParams(
            collective_id=0, has_side_effects=True, vmem_limit_bytes=62914560
        ),
    )(spectrum.reshape(ZQ * ZR, X, wrows, frames), basis, activations)
    return pl.pallas_call(
        write_out,
        out_shape=(
            jax.ShapeDtypeStruct(basis.shape, F32),
            jax.ShapeDtypeStruct(activations.shape, F32),
        ),
        in_specs=[vmem, vmem],
        out_specs=(anywhere, anywhere),
        scratch_shapes=[pltpu.SemaphoreType.DMA((2,))],
        compiler_params=pltpu.CompilerParams(vmem_limit_bytes=1 << 20),
    )(*fresh)


def solution(mesh):
    return jax.shard_map(
        per_device,
        mesh=mesh,
        in_specs=(P("freq", "frame"), P(("freq", "frame"), None), P(("frame", "freq"), None)),
        out_specs=(P(("freq", "frame"), None), P(("frame", "freq"), None)),
        check_vma=False,
    )
```

```python
import jax
import jax.numpy as jnp
from jax import lax
from jax.experimental import pallas as pl
from jax.experimental.pallas import tpu as pltpu
from jax.sharding import PartitionSpec as P

ITERS = 2
K = 128
X, ZR, ZQ = 4, 4, 2
Y, ZH, C = 4, 2, 2
SEMS = 224
GROUP = 2
PAIRS = ((2, 1, 3), (0,))
F32, BF16 = jnp.float32, jnp.bfloat16


def halves(value):
    high = value.astype(BF16)
    return high, (value - high.astype(F32)).astype(BF16)


def dot(left, right, contract_right):
    return lax.dot_general(
        left, right, (((1,), (contract_right,)), ((), ())), preferred_element_type=F32
    )


def outer(left, right):
    wide = dot(jnp.concatenate(left, axis=1), jnp.concatenate([right[0], right[0]], axis=1), 1)
    return wide + dot(left[0], right[1], 1)


def inner(left, right):
    wide = dot(left[0], jnp.concatenate(right, axis=1), 0)
    return wide[:, :K] + wide[:, K:] + dot(left[1], right[0], 0)


def fold8(value):
    return jnp.sum(value.reshape(-1, 8, K), axis=0)


def kernel(
    spec_hbm, basis_hbm, acts_hbm, basis_out, acts_out,
    raw, spec, spec_t, wp, gp,
    fcore, fcore_in, fy, fy_in, fz, fz_in,
    wacc, rx, rx_in, rt, rs, rs_in, rq, rq_in, ex_in, ez, ez_in,
    load_sem, send_sem, recv_sem,
):
    fr = lax.axis_index("frame")
    fq = lax.axis_index("freq")
    x, zl = lax.rem(fr, X), lax.div(fr, X)
    zr, zq = lax.rem(zl, ZR), lax.div(zl, ZR)
    c, yz = lax.rem(fq, C), lax.div(fq, C)
    y, zh = lax.rem(yz, Y), lax.div(yz, Y)
    wrows, grows = basis_hbm.shape[0], acts_hbm.shape[0]
    xbins, cframes = ZQ * ZR * wrows, ZH * Y * grows

    def frame_at(zq_, zr_, x_):
        return ((zq_ * ZR + zr_) * X + x_, fq)

    def freq_at(zh_, y_, c_):
        return (fr, (zh_ * Y + y_) * C + c_)

    def step(value, by, size):
        return lax.rem(value + by, size)

    core_peer = freq_at(zh, y, 1 - c)
    zh_peer = freq_at(1 - zh, y, c)
    zq_peer = frame_at(1 - zq, zr, x)
    y_peer = {d: freq_at(zh, step(y, d, Y), c) for d in (2, 1, 3)}
    steps = [(d, e) for d in (2, 1, 3, 0) for e in (2, 1, 3, 0) if d or e]
    xz_peer = {(d, e): frame_at(zq, step(zr, e, ZR), step(x, d, X)) for d, e in steps}
    peers = [zh_peer, zq_peer, *xz_peer.values(), *y_peer.values(), core_peer]

    barrier = pltpu.get_barrier_semaphore()
    for peer in peers:
        pl.semaphore_signal(barrier, inc=1, device_id=peer, device_id_type=pl.DeviceIdType.MESH)

    loads = [
        pltpu.make_async_copy(acts_hbm, gp.at[0, c, zh, y], load_sem.at[0]),
        pltpu.make_async_copy(basis_hbm, wp.at[0, x, zq, zr], load_sem.at[1]),
    ]
    for i in range(X):
        loads.append(pltpu.make_async_copy(spec_hbm.at[:, i], raw.at[i], load_sem.at[2 + i]))
    for load in loads:
        load.start()
    loads[0].wait()
    loads[1].wait()
    pl.semaphore_wait(barrier, len(peers))

    copies, drained = [], []

    def drain(last):
        for copy in copies[len(drained):-last]:
            copy.wait_send()
            drained.append(copy)

    def send(src, dst, peer):
        slot = len(copies)
        copy = pltpu.make_async_remote_copy(
            src_ref=src, dst_ref=dst, send_sem=send_sem.at[slot], recv_sem=recv_sem.at[slot],
            device_id=peer, device_id_type=pl.DeviceIdType.MESH,
        )
        copy.start()
        copies.append(copy)
        return copy

    def send_near(ref):
        return {d: send(ref, ref, y_peer[d]) for d in (2, 1, 3)}

    def send_plane(ref):
        return {at: send(ref, ref, xz_peer[at]) for at in steps}

    def wait_all(waits):
        for wait in waits:
            wait.wait_recv()

    def wait_near(near, part):
        passed = []
        for d in (1, 3, 2):
            near[d].wait_recv()
            there = part(step(y, Y - d, Y))
            passed.append(send(there, there, core_peer))
        return passed

    mine_w, mine_g = wp.at[0, x, zq, zr], gp.at[0, c, zh, y]
    far_g = send(mine_g, mine_g, zh_peer)
    far_w = send(mine_w, mine_w, zq_peer)
    near = send_near(mine_g)
    cross = [send(mine_g, mine_g, core_peer)]
    plane = send_plane(mine_w)
    for load in loads[2:]:
        load.wait()
    for i in range(X):
        turned = raw[i].reshape(xbins, C * cframes).T
        for j in range(C * ZH * Y):
            spec_t[i, j % C, pl.ds(j // C * grows, grows)] = turned[j * grows:(j + 1) * grows]
    cross += wait_near(near, lambda y_: gp.at[0, c, zh, y_])
    far_w.wait_recv()
    there = wp.at[0, x, 1 - zq, zr]
    plane_far = send_plane(there)
    far_g.wait_recv()
    wait_all(cross)
    there = gp.at[0, c, 1 - zh, y]
    far_near = send_near(there)
    cross = [send(there, there, core_peer)]
    wait_all(plane.values())
    cross += wait_near(far_near, lambda y_: gp.at[0, c, 1 - zh, y_])
    wait_all(plane_far.values())

    def acts_terms(it, c_, zh_, xs):
        w = halves(jnp.concatenate([wp[it, i].reshape(xbins, K) for i in xs], axis=0))
        if zh_ is None:
            g, rows = gp[it, c_].reshape(cframes, K), pl.ds(0, cframes)
        else:
            g, rows = gp[it, c_, zh_].reshape(Y * grows, K), pl.ds(zh_ * Y * grows, Y * grows)
        s = jnp.concatenate([spec_t[i, c_, rows] for i in xs], axis=1)
        return inner(halves(s / outer(halves(g), w)), w)

    def basis_terms(it, xs, c_):
        w = halves(jnp.concatenate([wp[it, i].reshape(xbins, K) for i in xs], axis=0))
        g = halves(gp[it + 1, c_].reshape(cframes, K))
        s = jnp.concatenate([spec[c_, i] for i in xs], axis=0)
        return inner(halves(s / outer(w, g)), g)

    half, tail = Y * grows, pl.ds(grows, 8)

    for it in range(ITERS):
        order = (0, 1) if it else (zh, 1 - zh)
        arrival = (0, 1) if it else (1 - zh, zh)
        others = [step(x, d, X) for d in (1, 3, 2)]

        def add_terms(c_, k, xs):
            terms = acts_terms(it, c_, order[k], xs)
            rows = pl.ds(0, half)
            fcore[it, c_, order[k], rows] = fcore[it, c_, order[k], rows] + terms if it else terms

        def send_core(k):
            rows = pl.ds(0, half if k else half + 8)
            return send(fcore.at[it, 1 - c, order[k], rows], fcore_in.at[it, order[k], rows], core_peer)

        def send_y(k, core):
            h, n = order[k], grows if k else grows + 8
            core.wait_recv()
            for i in range(Y):
                rows = pl.ds(i * grows, grows)
                fy[it, h, i, pl.ds(0, grows)] = fcore[it, c, h, rows] + fcore_in[it, h, rows]
                if k == 0:
                    rows = pl.ds(half, 8)
                    fy[it, h, i, tail] = fcore[it, c, h, rows] + fcore_in[it, h, rows]
            rows = pl.ds(0, n)
            return {
                d: send(fy.at[it, h, step(y, d, Y), rows], fy_in.at[it, h, d - 1, rows], y_peer[d])
                for d in (2, 1, 3)
            }

        def send_far(k, near):
            h, rows = order[k], pl.ds(0, grows if k else grows + 8)
            total = fy[it, h, y, rows]
            for d in (1, 3, 2):
                near[d].wait_recv()
                total = total + fy_in[it, h, d - 1, rows]
            fz[it, h, rows] = total
            return send(fz.at[it, h, rows], fz_in.at[it, h, rows], zh_peer)

        if it:
            wait_all(part[0, e] for part in plane_parts for e in range(1, ZR))
            for c_ in (1 - c, c):
                terms = acts_terms(it, c_, None, [x])
                for i in range(ZH):
                    fcore[it, c_, i, pl.ds(0, half)] = terms[i * half:(i + 1) * half]
            wait_all(part[at] for part in plane_parts for at in steps if at[0])
        sums = fold8(wp[it])
        for c_ in range(C):
            fcore[it, c_, order[0], pl.ds(half, 8)] = sums
        xs = others if it else [x, *others]
        add_terms(1 - c, 0, xs)
        core = [send_core(0)]
        if it:
            add_terms(1 - c, 1, xs)
            core.append(send_core(1))
            add_terms(c, 0, xs)
            near = [send_y(0, core[0])]
            add_terms(c, 1, xs)
        else:
            add_terms(c, 0, xs)
            wait_all(cross)
            add_terms(1 - c, 1, xs)
            core.append(send_core(1))
            near = [send_y(0, core[0])]
            add_terms(c, 1, xs)
        near.append(send_y(1, core[1]))
        far = [send_far(k, near[k]) for k in range(ZH)]
        drain(ZH)
        if it == 0:
            for i in range(X):
                for j in range(C):
                    spec[j, i] = spec_t[i, j].T
        near, cross = [], []
        for k in range(ZH):
            far[k].wait_recv()
            h = arrival[k]
            if k == 0:
                scale = jnp.sum(fz[it, order[0], tail] + fz_in[it, h, tail], axis=0)
            rows = pl.ds(0, grows)
            gp[it + 1, c, h, y] = gp[it, c, h, y] * (fz[it, h, rows] + fz_in[it, h, rows]) / scale
            mine = gp.at[it + 1, c, h, y]
            near.append(send_near(mine))
            cross.append(send(mine, mine, core_peer))
        if it + 1 == ITERS:
            acts_out[...] = gp[it + 1, c, zh, y]
        for k in range(ZH):
            cross += wait_near(near[k], lambda y_: gp.at[it + 1, c, arrival[k], y_])

        for i in range(0, X, GROUP):
            terms = basis_terms(it, range(i, i + GROUP), c)
            for j in range(GROUP):
                wacc[i + j] = terms[j * xbins:(j + 1) * xbins]
        sums = fold8(gp[it + 1, c])
        wait_all(cross)
        sums = sums + fold8(gp[it + 1, 1 - c])
        rt[it] = sums
        totals = {at: send(rt.at[it], rs_in.at[it, at[0], at[1]], xz_peer[at]) for at in steps}
        plane = {}
        sides = (1 - zq, zq) if it + 1 == ITERS else range(ZQ)
        for ds in PAIRS:
            xs = [step(x, d, X) for d in ds]
            both = basis_terms(it, xs, 1 - c)
            for n, x_ in enumerate(xs):
                terms = wacc[x_] + both[n * xbins:(n + 1) * xbins]
                rx[it, x_] = terms.reshape(ZQ, ZR, wrows, K)
            for k, j in enumerate(sides):
                for d, x_ in zip(ds, xs):
                    if it + 1 < ITERS:
                        for at in steps:
                            if at[0] == d:
                                src = rx.at[it, x_, j, step(zr, at[1], ZR)]
                                plane[k, at] = send(src, rx_in.at[at[0], j, at[1]], xz_peer[at])
                    elif d:
                        plane[k, d] = send(rx.at[it, x_, j], ex_in.at[d - 1, j], xz_peer[d, 0])
        for at in steps:
            totals[at].wait_recv()
            sums = sums + rs_in[it, at[0], at[1]]
        rs[it] = sums
        swap = send(rs.at[it], rs_in.at[it, 0, 0], zq_peer)
        if it + 1 < ITERS:
            far = []
            for j in range(ZQ):
                total = rx[it, x, j, zr]
                for at in sorted(steps):
                    plane[j, at].wait_recv()
                    total = total + rx_in[at[0], j, at[1]]
                rq[j] = total
                far.append(send(rq.at[j], rq_in.at[j], zq_peer))
            drain(1 + ZQ)
            swap.wait_recv()
            scale = jnp.sum(sums + rs_in[it, 0, 0], axis=0)
            plane_parts = []
            for j in range(ZQ):
                far[j].wait_recv()
                wp[it + 1, x, j, zr] = wp[it, x, j, zr] * (rq[j] + rq_in[j]) / scale
                plane_parts.append(send_plane(wp.at[it + 1, x, j, zr]))
        else:
            parts = {}
            for k, j in enumerate(sides):
                total = rx[it, x, j]
                for d in (1, 3, 2):
                    plane[k, d].wait_recv()
                    total = total + ex_in[d - 1, j]
                ez[j] = total
                for e in (2, 1, 3, 0):
                    if e or k == 0:
                        there = step(zr, e, ZR)
                        parts[k, e] = send(ez.at[j, there], ez_in.at[k, e], frame_at(j, there, x))
            drain(ZQ * ZR)
            swap.wait_recv()
            scale = jnp.sum(sums + rs_in[it, 0, 0], axis=0)
            total = ez[zq, zr]
            for k in (1, 0):
                for e in (1, 3, 2, 0):
                    if e or k == 0:
                        parts[k, e].wait_recv()
                        total = total + ez_in[k, e]
            basis_out[...] = wp[it, x, zq, zr] * total / scale

    for copy in copies[len(drained):]:
        copy.wait_send()


def write_out(basis_ref, acts_ref, basis_out, acts_out, sems):
    copies = [
        pltpu.make_async_copy(basis_ref, basis_out, sems.at[0]),
        pltpu.make_async_copy(acts_ref, acts_out, sems.at[1]),
    ]
    for copy in copies:
        copy.start()
    for copy in copies:
        copy.wait()


def per_device(spectrum, basis, activations):
    bins, frames = spectrum.shape
    wrows, grows = basis.shape[0], activations.shape[0]
    anywhere = pl.BlockSpec(memory_space=pl.ANY)
    vmem = pl.BlockSpec(memory_space=pltpu.VMEM)
    fresh = pl.pallas_call(
        kernel,
        out_shape=(
            pltpu.VMEM(basis.shape, F32),
            pltpu.VMEM(activations.shape, F32),
        ),
        in_specs=[anywhere] * 3,
        out_specs=(vmem, vmem),
        scratch_shapes=[
            pltpu.VMEM((X, ZQ * ZR, wrows, frames), F32),
            pltpu.VMEM((C, X, bins // X, frames // C), F32),
            pltpu.VMEM((X, C, frames // C, bins // X), F32),
            pltpu.VMEM((ITERS + 1, X, ZQ, ZR, wrows, K), F32),
            pltpu.VMEM((ITERS + 1, C, ZH, Y, grows, K), F32),
            pltpu.VMEM((ITERS, C, ZH, Y * grows + 8, K), F32),
            pltpu.VMEM((ITERS, ZH, Y * grows + 8, K), F32),
            pltpu.VMEM((ITERS, ZH, Y, grows + 8, K), F32),
            pltpu.VMEM((ITERS, ZH, Y - 1, grows + 8, K), F32),
            pltpu.VMEM((ITERS, ZH, grows + 8, K), F32),
            pltpu.VMEM((ITERS, ZH, grows + 8, K), F32),
            pltpu.VMEM((X, bins // X, K), F32),
            pltpu.VMEM((ITERS, X, ZQ, ZR, wrows, K), F32),
            pltpu.VMEM((X, ZQ, ZR, wrows, K), F32),
            pltpu.VMEM((ITERS, 8, K), F32),
            pltpu.VMEM((ITERS, 8, K), F32),
            pltpu.VMEM((ITERS, X, ZR, 8, K), F32),
            pltpu.VMEM((ZQ, wrows, K), F32),
            pltpu.VMEM((ZQ, wrows, K), F32),
            pltpu.VMEM((X - 1, ZQ, ZR, wrows, K), F32),
            pltpu.VMEM((ZQ, ZR, wrows, K), F32),
            pltpu.VMEM((ZQ, ZR, wrows, K), F32),
            pltpu.SemaphoreType.DMA((2 + X,)),
            pltpu.SemaphoreType.DMA((SEMS,)),
            pltpu.SemaphoreType.DMA((SEMS,)),
        ],
        compiler_params=pltpu.CompilerParams(
            collective_id=0, has_side_effects=True, vmem_limit_bytes=62914560
        ),
    )(spectrum.reshape(ZQ * ZR, X, wrows, frames), basis, activations)
    return pl.pallas_call(
        write_out,
        out_shape=(
            jax.ShapeDtypeStruct(basis.shape, F32),
            jax.ShapeDtypeStruct(activations.shape, F32),
        ),
        in_specs=[vmem, vmem],
        out_specs=(anywhere, anywhere),
        scratch_shapes=[pltpu.SemaphoreType.DMA((2,))],
        compiler_params=pltpu.CompilerParams(vmem_limit_bytes=1 << 20),
    )(*fresh)


def solution(mesh):
    return jax.shard_map(
        per_device,
        mesh=mesh,
        in_specs=(P("freq", "frame"), P(("freq", "frame"), None), P(("frame", "freq"), None)),
        out_specs=(P(("freq", "frame"), None), P(("frame", "freq"), None)),
        check_vma=False,
    )
```
